768 devices in a mesh: section: 8 (over x, core), seq: 32 (over z_lo, y), head: 3 (over z_hi).
Axes of the slice: x: 4, y: 8, z: 12 (z_hi: 3, z_lo: 4; z = z_hi * 4 + z_lo), core: 2. Of those that a mesh axis runs over, the one named last changes fastest.
Arguments:
- queries: bfloat16 [8, 4096, 2304], P('section', 'seq', 'head'), may hold values from -240 to 240
- grad_out: bfloat16 [8, 4096, 2304], P('section', 'seq', 'head'), may hold values from -96 to 96
- keys: bfloat16 [8, 2048, 1152], P('section', 'seq', 'head'), may hold values from -6 to 6
- values: bfloat16 [8, 2048, 1152], P('section', 'seq', 'head'), may hold values from -6 to 6
- proj_query: bfloat16 [8, 5376, 2304], P('section', None, 'head'), may hold values from -0.125 to 0.125
- section_span: int32 [8], replicated, may hold values from 0 to 7, each once
- span_prefix: int32 [8], replicated, may hold values from 1024 to 2048, as said below
Outputs:
- grad_input: bfloat16 [8, 5376, 4096], P('section', 'head', 'seq')
- grad_key: bfloat16 [8, 2048, 1152], P('section', 'seq', 'head')
- grad_value: bfloat16 [8, 2048, 1152], P('section', 'seq', 'head')
The draws below stay inside these ranges and needn't reach their ends.
Inputs may be any that keep to these rules, and one draw needn't show every extreme that they name: `span_prefix`: some entry equals 2048 in every draw.
All inputs are finite; a program needn't handle non-finite values.
Results may differ from the reference program's by a relative error of at most 0.023.
Values may be sent and summed in bfloat16 or wider, within the bound.
A program may use at most 64 MiB of HBM per device.

```python
import jax
import jax.numpy as jnp
from jax import lax

D = 5376
HD = 128
Q_DEV = 128
KV_HEADS = 9
QH = 18
ROWS = 4096
PREFIX = 2048
SECTIONS = 8
N_SEQ = 32


def draw_pair(key):
    base_q = jax.random.truncated_normal(jax.random.fold_in(key, 11), -6.0, 6.0, (SECTIONS, ROWS, QH * HD), jnp.float32)
    base_k = jax.random.truncated_normal(jax.random.fold_in(key, 12), -6.0, 6.0, (SECTIONS, PREFIX, KV_HEADS * HD), jnp.float32)
    return (base_q, base_k)


def draw_queries(key, part):
    return draw_pair(key)[0].astype(jnp.bfloat16)


def draw_keys(key, part):
    return draw_pair(key)[1].astype(jnp.bfloat16)


def draw_span_prefix(key, part):
    lengths = jax.random.randint(jax.random.fold_in(key, 21), (SECTIONS,), PREFIX // 2, PREFIX + 1)
    where_full = jax.random.randint(jax.random.fold_in(key, 22), (), 0, SECTIONS)
    return jnp.where(jnp.arange(SECTIONS) == where_full, PREFIX, lengths).astype(jnp.int32)


def block_scale(key, extent, pieces, low, high):
    loudness = 1.0
    for axis_at, shards_of in pieces:
        draws = jax.random.uniform(jax.random.fold_in(jax.random.fold_in(key, 6), axis_at), (shards_of,), jnp.float32, low / len(pieces), high / len(pieces))
        loudness = loudness * jnp.repeat(jnp.exp(draws), extent[axis_at] // shards_of).reshape((-1,) + (1,) * (len(extent) - 1 - axis_at))
    return loudness


def gaussian(key, shape, width, most, pieces=(), kind=jnp.bfloat16):
    entries = width * jax.random.normal(key, shape, jnp.float32)
    if pieces:
        entries = entries * block_scale(key, shape, pieces, -0.22, 0.18)
    return jnp.clip(entries, -most, most).astype(kind)


def setup_inputs(seed: int = 0) -> dict:
    key_list = jax.random.split(jax.random.key(seed), 8)
    return {
        "queries": draw_queries(jax.random.fold_in(key_list[7], 71), 0),
        "grad_out": gaussian(key_list[1], (SECTIONS, ROWS, QH * HD), 16.0, 96.0, ((0, 8), (1, 32), (2, 3))),
        "keys": draw_keys(jax.random.fold_in(key_list[7], 71), 0),
        "values": gaussian(key_list[3], (SECTIONS, PREFIX, KV_HEADS * HD), 1.0, 6.0, ((0, 8), (1, 32), (2, 3))),
        "proj_query": gaussian(key_list[4], (SECTIONS, D, QH * HD), (QH * HD) ** -0.5, 0.125, ((0, 8), (2, 3))),
        "section_span": jax.random.permutation(key_list[5], SECTIONS).astype(jnp.int32),
        "span_prefix": draw_span_prefix(jax.random.fold_in(key_list[7], 71), 0),
    }


query_scale = 168.0 ** -0.5


def to_groups(matrix):
    count = matrix.shape[1] // (2 * HD)
    return matrix.reshape(matrix.shape[0], count, 2, HD).transpose(1, 2, 0, 3).reshape(count, 2 * matrix.shape[0], HD)


def from_groups(stacked):
    count = stacked.shape[0]
    rows_half = stacked.shape[1] // 2
    return stacked.reshape(count, 2, rows_half, HD).transpose(2, 0, 1, 3).reshape(rows_half, count * 2 * HD)


def kv_groups(matrix):
    return matrix.reshape(matrix.shape[0], matrix.shape[1] // HD, HD).transpose(1, 0, 2)


def kv_flat(stacked):
    return stacked.transpose(1, 0, 2).reshape(stacked.shape[1], stacked.shape[0] * HD)


def contract_rows(left, right):
    return lax.dot_general(left, right, (((0,), (0,)), ((), ())), preferred_element_type=jnp.float32)


def group_pass(q_group, d_group, k_group, v_group, live):
    scores = query_scale * jnp.dot(q_group, k_group.T, preferred_element_type=jnp.float32)
    scores = jnp.where(live[None, :], scores, jnp.float32(-1e30))
    top = jnp.max(scores, axis=1, keepdims=True)
    lse = top + jnp.log(jnp.sum(jnp.exp(scores - top), axis=1, keepdims=True))
    probs = jnp.where(live[None, :], jnp.exp(scores - lse), jnp.float32(0.0))
    probs_low = probs.astype(jnp.bfloat16)
    attn = jnp.dot(probs_low, v_group, preferred_element_type=jnp.float32)
    delta = jnp.sum(d_group.astype(jnp.float32) * attn, axis=1, keepdims=True)
    dprobs = jnp.dot(d_group, v_group.T, preferred_element_type=jnp.float32)
    dscores = (probs * (dprobs - delta)).astype(jnp.bfloat16)
    grad_q = (query_scale * jnp.dot(dscores, k_group, preferred_element_type=jnp.float32)).astype(jnp.bfloat16)
    grad_k = query_scale * contract_rows(dscores, q_group)
    grad_v = contract_rows(probs_low, d_group)
    return grad_q, grad_k, grad_v


def rounded(matrix):
    return lax.optimization_barrier(matrix.astype(jnp.bfloat16)).astype(jnp.float32)


def reference(queries, grad_out, keys, values, proj_query, section_span, span_prefix):
    incoming = jnp.roll(grad_out, -1, axis=0)

    def one_section(index):
        length = span_prefix[section_span[index]]
        live = jnp.arange(PREFIX, dtype=jnp.int32) < length
        k_groups = kv_groups(keys[index])
        v_groups = kv_groups(values[index])
        q_section = queries[index]
        d_section = incoming[index]

        def one_block(totals, block):
            start = (block * Q_DEV).astype(jnp.int32)
            q_groups = to_groups(lax.dynamic_slice_in_dim(q_section, start, Q_DEV, 0))
            d_groups = to_groups(lax.dynamic_slice_in_dim(d_section, start, Q_DEV, 0))

            def per_group(members):
                return group_pass(members[0], members[1], members[2], members[3], live)

            grad_q, grad_k, grad_v = lax.map(per_group, (q_groups, d_groups, k_groups, v_groups))
            key_sum = totals[0] + rounded(kv_flat(grad_k))
            value_sum = totals[1] + rounded(kv_flat(grad_v))
            return (key_sum, value_sum), from_groups(grad_q)

        zeros = jnp.zeros((PREFIX, KV_HEADS * HD), jnp.float32)
        totals, blocks = lax.scan(one_block, (zeros, zeros), jnp.arange(N_SEQ, dtype=jnp.int32))
        grad_query = blocks.reshape(ROWS, QH * HD)
        grad_input = lax.dot_general(proj_query[index], grad_query, (((1,), (1,)), ((), ())), preferred_element_type=jnp.float32)
        return grad_input.astype(jnp.bfloat16), totals[0].astype(jnp.bfloat16), totals[1].astype(jnp.bfloat16)

    grad_input, grad_key, grad_value = lax.map(one_section, jnp.arange(SECTIONS, dtype=jnp.int32))
    return grad_input, grad_key, grad_value
```

```python
import functools
import math

import jax
import jax.numpy as jnp
from jax import lax
from jax.experimental import pallas as pl
from jax.experimental.pallas import tpu as pltpu
from jax.sharding import Mesh
from jax.sharding import PartitionSpec as P

HD = 128
SEQ = ("seq_0", "seq_1")
NZ = 4
NY = 8
SCALE = 168.0 ** (-0.5)
SCALE_LOG2 = SCALE * math.log2(math.e)
CHUNK = 256
VMEM = pltpu.VMEM
DMA = pltpu.SemaphoreType.DMA


def column_mates(z):
    return (z + 1 - 2 * (z % 2), (z + 2) % NZ, NZ - 1 - z)


def remote(src, dst, send, recv, target):
    return pltpu.make_async_remote_copy(
        src_ref=src,
        dst_ref=dst,
        send_sem=send,
        recv_sem=recv,
        device_id=target,
        device_id_type=pl.DeviceIdType.MESH,
    )


def greet(targets):
    barrier = pltpu.get_barrier_semaphore()
    for target in targets:
        pl.semaphore_signal(
            barrier, inc=1, device_id=target, device_id_type=pl.DeviceIdType.MESH
        )
    pl.semaphore_wait(barrier, len(targets))


def gather_kernel(k_ref, v_ref, d_ref, k_all, v_all, d_new, send, recv, shift_sem, own_sem):
    z = lax.axis_index("seq_0")
    y = lax.axis_index("seq_1")
    s = lax.axis_index("section")
    right, left = (y + 1) % NY, (y + NY - 1) % NY
    mates = column_mates(z)
    down, up = (s + 7) % 8, (s + 1) % 8
    greet(
        [{"seq_1": right}, {"seq_1": left}]
        + [{"seq_0": m} for m in mates]
        + [{"section": down}, {"section": up}]
    )
    own = (k_ref, v_ref)
    full = (k_all, v_all)
    sent = []

    def push(src, kv, z0, y0, target):
        copy = remote(src, full[kv].at[z0, y0], send.at[len(sent)], recv.at[kv, z0, y0], target)
        copy.start()
        sent.append(copy)

    def arrived(kv, z0, y0):
        block = full[kv].at[z0, y0]
        remote(block, block, send.at[0], recv.at[kv, z0, y0], {"seq_1": right}).wait_recv()

    for kv in range(2):
        for m in mates:
            push(own[kv], kv, z, y, {"seq_0": m})
    for kv in range(2):
        push(own[kv], kv, z, y, {"seq_1": right})
        push(own[kv], kv, z, y, {"seq_1": left})
    shift = remote(d_ref, d_new, shift_sem.at[0], shift_sem.at[1], {"section": down})
    shift.start()
    here = [pltpu.make_async_copy(own[kv], full[kv].at[z, y], own_sem.at[kv]) for kv in range(2)]
    for copy in here:
        copy.start()
    for m in mates:
        for kv in range(2):
            arrived(kv, m, y)
            push(full[kv].at[m, y], kv, m, y, {"seq_1": right})
            push(full[kv].at[m, y], kv, m, y, {"seq_1": left})
    reach = ((4, 3), (3, 4))
    for hop in range(1, 5):
        for m in (z,) + mates:
            for kv in range(2):
                if hop <= reach[kv][0]:
                    y0 = (y + NY - hop) % NY
                    arrived(kv, m, y0)
                    if hop < reach[kv][0]:
                        push(full[kv].at[m, y0], kv, m, y0, {"seq_1": right})
                if hop <= reach[kv][1]:
                    y0 = (y + hop) % NY
                    arrived(kv, m, y0)
                    if hop < reach[kv][1]:
                        push(full[kv].at[m, y0], kv, m, y0, {"seq_1": left})
    for copy in sent:
        copy.wait_send()
    for copy in here:
        copy.wait()
    shift.wait()


def gathered(k, v, d):
    count = 62
    return pl.pallas_call(
        gather_kernel,
        out_shape=(
            jax.ShapeDtypeStruct((NZ, NY) + k.shape, k.dtype),
            jax.ShapeDtypeStruct((NZ, NY) + v.shape, v.dtype),
            jax.ShapeDtypeStruct(d.shape, d.dtype),
        ),
        in_specs=[pl.BlockSpec(memory_space=VMEM)] * 3,
        out_specs=(pl.BlockSpec(memory_space=VMEM),) * 3,
        scratch_shapes=[DMA((count,)), DMA((2, NZ, NY)), DMA((2,)), DMA((2,))],
        compiler_params=pltpu.CompilerParams(collective_id=0, has_side_effects=True),
        name="gather_kv",
    )(k, v, d)


def dot_nt(a, b):
    return lax.dot_general(a, b, (((1,), (1,)), ((), ())), preferred_element_type=jnp.float32)


def dot_nn(a, b):
    return lax.dot_general(a, b, (((1,), (0,)), ((), ())), preferred_element_type=jnp.float32)


def dot_tn(a, b):
    return lax.dot_general(a, b, (((0,), (0,)), ((), ())), preferred_element_type=jnp.float32)


def by_eight(x):
    return x.reshape(x.shape[0] // 8, 8, x.shape[1])


def attention_kernel(len_ref, q_ref, d_ref, k_ref, v_ref, gq_ref, gk_ref, gv_ref, s_buf, p_buf):
    length = len_ref[0]
    prefix = k_ref.shape[0]
    two = lambda ref: jnp.concatenate([ref[:, :HD], ref[:, HD:]], axis=0)
    q2, d2 = two(q_ref), two(d_ref)
    cols = q2.shape[0]
    chunks = [pl.ds(at, CHUNK) for at in range(0, prefix, CHUNK)]
    top = jnp.full((8, cols), -1e30, jnp.float32)
    for c, rows in enumerate(chunks):
        s = dot_nt(k_ref[rows, :], q2)
        t = c * CHUNK + lax.broadcasted_iota(jnp.int32, s.shape, 0)
        s = jnp.where(t < length, s, jnp.float32(-1e30))
        s_buf[rows, :] = s
        top = jnp.maximum(top, by_eight(s).max(axis=0))
    top = top.max(axis=0, keepdims=True)
    total = jnp.zeros((8, cols), jnp.float32)
    dots = jnp.zeros((8, cols), jnp.float32)
    for rows in chunks:
        e = jnp.exp2((s_buf[rows, :] - top) * SCALE_LOG2)
        dp = dot_nt(v_ref[rows, :], d2)
        s_buf[rows, :] = e
        p_buf[rows, :] = dp
        total = total + by_eight(e).sum(axis=0)
        dots = dots + by_eight(e * dp).sum(axis=0)
    inv = 1.0 / total.sum(axis=0, keepdims=True)
    delta = dots.sum(axis=0, keepdims=True) * inv
    gq = jnp.zeros((HD, cols), jnp.float32)
    for rows in chunks:
        p = s_buf[rows, :] * inv
        ds = (p * (p_buf[rows, :] - delta)).astype(jnp.bfloat16)
        gv_ref[rows, :] = dot_nn(p.astype(jnp.bfloat16), d2).astype(jnp.bfloat16)
        gk_ref[rows, :] = (SCALE * dot_nn(ds, q2)).astype(jnp.bfloat16)
        gq = gq + dot_tn(k_ref[rows, :], ds)
    gq = (SCALE * gq).astype(jnp.bfloat16)
    half = cols // 2
    gq_ref[:HD, :] = gq[:, :half]
    gq_ref[HD:, :] = gq[:, half:]


def attention(length, q, d, k, v):
    rows, width = q.shape
    groups = width // (2 * HD)
    prefix = k.shape[0]
    row_spec = pl.BlockSpec((rows, 2 * HD), lambda g, n: (0, g))
    key_spec = pl.BlockSpec((prefix, HD), lambda g, n: (0, g))
    return pl.pallas_call(
        attention_kernel,
        out_shape=(
            jax.ShapeDtypeStruct((width, rows), jnp.bfloat16),
            jax.ShapeDtypeStruct(k.shape, jnp.bfloat16),
            jax.ShapeDtypeStruct(v.shape, jnp.bfloat16),
        ),
        grid_spec=pltpu.PrefetchScalarGridSpec(
            num_scalar_prefetch=1,
            grid=(groups,),
            in_specs=[row_spec, row_spec, key_spec, key_spec],
            out_specs=(pl.BlockSpec((2 * HD, rows), lambda g, n: (g, 0)), key_spec, key_spec),
            scratch_shapes=[
                VMEM((prefix, 2 * rows), jnp.float32),
                VMEM((prefix, 2 * rows), jnp.float32),
            ],
        ),
        name="attention_backward",
    )(length, q, d, k, v)


def reduce_kernel(
    w_ref, gq_ref, gk_ref, gv_ref, gi_out, gk_out, gv_out,
    gi_send, gi_recv, gi_own, ring, mine, line,
    gi_sem, ring_send, ring_recv, line_send, line_recv,
):
    z = lax.axis_index("seq_0")
    y = lax.axis_index("seq_1")
    h = lax.axis_index("head")
    right, left = (y + 1) % NY, (y + NY - 1) % NY
    mates = column_mates(z)
    others = ((h + 1) % 3, (h + 2) % 3)
    greet(
        [{"seq_1": right}, {"seq_1": left}]
        + [{"seq_0": m} for m in mates]
        + [{"head": o} for o in others]
    )
    terms = (gk_ref, gv_ref)
    chains = ((0, 1, 4, 0), (1, -1, 4, 4), (0, -1, 3, 8), (1, 1, 3, 11))
    sent = []

    def ring_copy(chain, hop, src):
        kv, way, hops, slot = chain
        i = slot + hop
        return remote(
            src, ring.at[i], ring_send.at[i], ring_recv.at[i], {"seq_1": right if way > 0 else left}
        )

    for chain in chains:
        kv, way, hops, slot = chain
        owner = (y + NY + way * hops) % NY
        copy = ring_copy(chain, 0, terms[kv].at[:, owner])
        copy.start()
        sent.append(copy)

    size = gi_own.shape[0]
    gq = gq_ref[...]
    gi_copies = []
    for i, o in enumerate(others):
        rows = pl.ds(pl.multiple_of(o * size, size), size)
        gi_send[i] = dot_nn(w_ref[rows, :], gq).astype(jnp.bfloat16)
        copy = remote(
            gi_send.at[i], gi_recv.at[i], gi_sem.at[0, i], gi_sem.at[1, i], {"head": o}
        )
        copy.start()
        gi_copies.append(copy)
    gi_own[...] = dot_nn(w_ref[pl.ds(pl.multiple_of(h * size, size), size), :], gq)

    for hop in range(4):
        for chain in chains:
            kv, way, hops, slot = chain
            if hop >= hops:
                continue
            i = slot + hop
            ring_copy(chain, hop, ring.at[i]).wait_recv()
            if hop < hops - 1:
                owner = (y + NY + way * (hops - 1 - hop)) % NY
                ring[i] = (
                    ring[i].astype(jnp.float32) + terms[kv][:, owner].astype(jnp.float32)
                ).astype(jnp.bfloat16)
                copy = ring_copy(chain, hop + 1, ring.at[i])
                copy.start()
                sent.append(copy)
    ends = ((3, 10), (13, 7))
    line_copies = []
    for kv in range(2):
        a, b = ends[kv]
        mine[kv] = (
            ring[a].astype(jnp.float32)
            + ring[b].astype(jnp.float32)
            + terms[kv][:, y].astype(jnp.float32)
        ).astype(jnp.bfloat16)
        for i, m in enumerate(mates):
            copy = remote(
                mine.at[kv, m], line.at[kv, i], line_send.at[kv, i], line_recv.at[kv, i], {"seq_0": m}
            )
            copy.start()
            line_copies.append(copy)
    for i in range(2):
        gi_copies[i].wait_recv()
    gi_out[...] = (
        gi_own[...] + gi_recv[0].astype(jnp.float32) + gi_recv[1].astype(jnp.float32)
    ).astype(jnp.bfloat16)
    for copy in line_copies:
        copy.wait_recv()
    for kv, out in enumerate((gk_out, gv_out)):
        out[...] = (
            mine[kv, z].astype(jnp.float32)
            + line[kv, 0].astype(jnp.float32)
            + line[kv, 1].astype(jnp.float32)
            + line[kv, 2].astype(jnp.float32)
        ).astype(jnp.bfloat16)
    for copy in sent + line_copies + gi_copies:
        copy.wait_send()


def reduced(w, gq, gk, gv):
    features, rows = w.shape[0] // 3, gq.shape[1]
    block = gk.shape[2:]
    return pl.pallas_call(
        reduce_kernel,
        out_shape=(
            jax.ShapeDtypeStruct((features, rows), jnp.bfloat16),
            jax.ShapeDtypeStruct(block, jnp.bfloat16),
            jax.ShapeDtypeStruct(block, jnp.bfloat16),
        ),
        in_specs=[pl.BlockSpec(memory_space=VMEM)] * 4,
        out_specs=(pl.BlockSpec(memory_space=VMEM),) * 3,
        scratch_shapes=[
            VMEM((2, features, rows), jnp.bfloat16),
            VMEM((2, features, rows), jnp.bfloat16),
            VMEM((features, rows), jnp.float32),
            VMEM((14, NZ) + block, jnp.bfloat16),
            VMEM((2, NZ) + block, jnp.bfloat16),
            VMEM((2, 3) + block, jnp.bfloat16),
            DMA((2, 2)),
            DMA((14,)),
            DMA((14,)),
            DMA((2, 3)),
            DMA((2, 3)),
        ],
        compiler_params=pltpu.CompilerParams(collective_id=1, has_side_effects=True),
        name="project_and_reduce",
    )(w, gq, gk, gv)


def on_device(queries, grad_out, keys, values, proj_query, section_span, span_prefix):
    length = span_prefix[section_span[lax.axis_index("section")]].reshape(1)
    k_all, v_all, incoming = gathered(keys[0], values[0], grad_out[0])
    flat = lambda a: a.reshape(-1, a.shape[-1])
    gq, gk, gv = attention(length, queries[0], incoming, flat(k_all), flat(v_all))
    gi, gk, gv = reduced(proj_query[0], gq, gk.reshape(k_all.shape), gv.reshape(v_all.shape))
    return gi[None], gk[None], gv[None]


def solution(mesh):
    split = Mesh(
        mesh.devices.reshape(mesh.shape["section"], NZ, NY, mesh.shape["head"]),
        ("section", "seq_0", "seq_1", "head"),
    )
    in_specs = (
        P("section", SEQ, "head"),
        P("section", SEQ, "head"),
        P("section", SEQ, "head"),
        P("section", SEQ, "head"),
        P("section", None, "head"),
        P(),
        P(),
    )
    out_specs = (P("section", "head", SEQ), P("section", SEQ, "head"), P("section", SEQ, "head"))
    return jax.shard_map(
        on_device, mesh=split, in_specs=in_specs, out_specs=out_specs, check_vma=False
    )
```

```python
import functools
import math

import jax
import jax.numpy as jnp
from jax import lax
from jax.experimental import pallas as pl
from jax.experimental.pallas import tpu as pltpu
from jax.sharding import Mesh
from jax.sharding import PartitionSpec as P

HD = 128
SEQ = ("seq_0", "seq_1")
NZ = 4
NY = 8
NS = 8
NH = 3
GROUPS = 3
SCALE = 168.0 ** (-0.5)
SCALE_LOG2 = SCALE * math.log2(math.e)
LEAD = 16
VMEM = pltpu.VMEM
SMEM = pltpu.SMEM
DMA = pltpu.SemaphoreType.DMA
BF16 = jnp.bfloat16
F32 = jnp.float32


def column_mates(z):
    return (z + 1 - 2 * (z % 2), (z + 2) % NZ, NZ - 1 - z)


def remote(src, dst, send, recv, target):
    return pltpu.make_async_remote_copy(
        src_ref=src,
        dst_ref=dst,
        send_sem=send,
        recv_sem=recv,
        device_id=target,
        device_id_type=pl.DeviceIdType.MESH,
    )


def dot_nt(a, b):
    return lax.dot_general(a, b, (((1,), (1,)), ((), ())), preferred_element_type=F32)


def dot_nn(a, b):
    return lax.dot_general(a, b, (((1,), (0,)), ((), ())), preferred_element_type=F32)


def dot_tn(a, b):
    return lax.dot_general(a, b, (((0,), (0,)), ((), ())), preferred_element_type=F32)


def by_eight(x):
    return x.reshape(x.shape[0] // 8, 8, x.shape[1])


def flat(x):
    return x.reshape(x.shape[0] * x.shape[1], x.shape[2])


def tick_kernel(
    span_ref, prefix_ref, q_ref, d_ref, k_ref, v_ref, w_ref,
    gi_out, gk_out, gv_out,
    k_all, v_all, d_new, q2, d2, w_own, w_edge,
    e_buf, dp_buf, stats, ds_buf, p_buf, gk, gv,
    gq, gq_in, gi_send, gi_recv, gi_own, ring, mine, line,
    send, recv_a, recv_b, misc, gq_send, gq_recv, gi_ssem, gi_rsem,
    ring_send, ring_recv, line_send, line_recv,
):
    z = lax.axis_index("seq_0")
    y = lax.axis_index("seq_1")
    h = lax.axis_index("head")
    s = lax.axis_index("section")
    right, left = (y + 1) % NY, (y + NY - 1) % NY
    mates = column_mates(z)
    lower, upper = (s + NS - 1) % NS, (s + 1) % NS
    before, after = (h + NH - 1) % NH, (h + 1) % NH
    top_edge = z // (NZ - 1)
    is_edge = (z % (NZ - 1)) == 0
    goal = (h + NH - 1 + 2 * top_edge) % NH

    w_size = w_own.shape[0]
    w_copies = [
        pltpu.make_async_copy(
            w_ref.at[pl.ds(pl.multiple_of(at * w_size, w_size), w_size), :], buf, misc.at[2 + i]
        )
        for i, (at, buf) in enumerate(((h, w_own), (goal, w_edge)))
    ]
    for copy in w_copies:
        copy.start()

    barrier = pltpu.get_barrier_semaphore()

    def greet(target):
        pl.semaphore_signal(
            barrier, inc=1, device_id=target, device_id_type=pl.DeviceIdType.MESH
        )

    for target in (
        [{"seq_1": right}, {"seq_1": left}]
        + [{"seq_0": m} for m in mates]
        + [{"section": lower}, {"section": upper}]
        + [{"seq_0": z * 0 + NZ - 1, "head": before}, {"seq_0": z * 0, "head": after}]
    ):
        greet(target)

    @pl.when(is_edge)
    def _():
        for j in range(NZ):
            greet({"seq_0": z * 0 + j, "head": goal})

    pl.semaphore_wait(barrier, 9 + 4 * jnp.where(is_edge, 1, 0))

    own = (k_ref, v_ref)
    full = (k_all, v_all)
    size = k_ref.shape[0]
    rows_of = (pl.ds(0, LEAD), pl.ds(LEAD, size - LEAD))
    recv = (recv_a, recv_b)
    sent = []

    def part(kv, cls, z0, y0):
        return full[kv].at[y0, z0, rows_of[cls]]

    def push(src, kv, cls, z0, y0, target):
        copy = remote(
            src, part(kv, cls, z0, y0), send.at[len(sent)], recv[cls].at[kv, y0, z0], target
        )
        copy.start()
        sent.append(copy)

    def arrived(kv, cls, z0, y0):
        block = part(kv, cls, z0, y0)
        remote(block, block, send.at[0], recv[cls].at[kv, y0, z0], {"seq_1": right}).wait_recv()

    both = ({"seq_1": right}, {"seq_1": left})
    for kv in range(2):
        for target in both:
            push(own[kv].at[rows_of[0]], kv, 0, z, y, target)
    for m in mates:
        for kv in range(2):
            push(own[kv].at[rows_of[1]], kv, 1, z, y, {"seq_0": m})
    for kv in range(2):
        for target in both:
            push(own[kv].at[rows_of[1]], kv, 1, z, y, target)
    for m in mates:
        for kv in range(2):
            push(own[kv].at[rows_of[0]], kv, 0, z, y, {"seq_0": m})
    shift = remote(d_ref, d_new, misc.at[0], misc.at[1], {"section": lower})
    shift.start()
    for kv in range(2):
        full[kv][y, z] = own[kv][...]

    length = prefix_ref[span_ref[s]]

    def halves(ref, g):
        return jnp.concatenate(
            [ref[:, 2 * g * HD : (2 * g + 1) * HD], ref[:, (2 * g + 1) * HD : (2 * g + 2) * HD]],
            axis=0,
        )

    for g in range(GROUPS):
        q2[g] = halves(q_ref, g)

    def chunk_of(ref, y0, g):
        return flat(ref[y0, :, :, g * HD : (g + 1) * HD])

    def scores_unit(y0, g):
        sc = dot_nt(chunk_of(k_all, y0, g), q2[g])
        dp = dot_nt(chunk_of(v_all, y0, g), d2[g])
        n = sc.shape[0] // 2
        i = lax.broadcasted_iota(jnp.int32, (n, sc.shape[1]), 0)
        t = i + jnp.where(i >= size, (NY - 1) * size, 0)
        live = t < length - 2 * NY * size - y0 * size
        sc = jnp.concatenate([sc[:n], jnp.where(live, sc[n:], F32(-1e30))], axis=0)
        m = by_eight(sc).max(axis=0).max(axis=0, keepdims=True)
        e = jnp.exp2((sc - m) * SCALE_LOG2)
        e_buf[g, y0] = e
        dp_buf[g, y0] = dp
        stats[0, g, y0] = m
        stats[1, g, y0] = by_eight(e).sum(axis=0).sum(axis=0, keepdims=True)
        stats[2, g, y0] = by_eight(e * dp).sum(axis=0).sum(axis=0, keepdims=True)

    for m in mates:
        for kv in range(2):
            arrived(kv, 1, m, y)
            for target in both:
                push(part(kv, 1, m, y), kv, 1, m, y, target)
    shift.wait_recv()
    for g in range(GROUPS):
        d2[g] = halves(d_new, g)

    reach = ((4, 3), (3, 4))
    todo = [y]
    for hop in range(1, 5):
        y_r, y_l = (y + NY - hop) % NY, (y + hop) % NY
        for kv in range(2):
            for way, y0 in enumerate((y_r, y_l)):
                if hop <= reach[kv][way]:
                    arrived(kv, 0, z, y0)
                    if hop < reach[kv][way]:
                        push(part(kv, 0, z, y0), kv, 0, z, y0, both[way])
                    for m in mates:
                        push(part(kv, 0, z, y0), kv, 0, z, y0, {"seq_0": m})
        units = []
        for y0 in todo:
            for kv in range(2):
                for m in mates:
                    arrived(kv, 0, m, y0)
            units += [(y0, g) for g in range(GROUPS)]
        for m in (z,) + mates:
            for kv in range(2):
                for way, y0 in enumerate((y_r, y_l)):
                    if hop <= reach[kv][way]:
                        arrived(kv, 1, m, y0)
                        if hop < reach[kv][way]:
                            push(part(kv, 1, m, y0), kv, 1, m, y0, both[way])
            for unit in units[:2]:
                scores_unit(*unit)
            units = units[2:]
        todo = [y_r, y_l] if hop < 4 else [y_r]
    for y0 in todo:
        for kv in range(2):
            for m in mates:
                arrived(kv, 0, m, y0)
        for g in range(GROUPS):
            scores_unit(y0, g)

    for g in range(GROUPS):
        m_c = [stats[0, g, c] for c in range(NY)]
        top = functools.reduce(jnp.maximum, m_c)
        f_c = [jnp.exp2((m - top) * SCALE_LOG2) for m in m_c]
        inv = 1.0 / sum(f * stats[1, g, c] for c, f in enumerate(f_c))
        delta = sum(f * stats[2, g, c] for c, f in enumerate(f_c)) * inv
        total = jnp.zeros((HD, q2.shape[1]), F32)
        for c in range(NY):
            p = e_buf[g, c] * (f_c[c] * inv)
            ds = (p * (dp_buf[g, c] - delta)).astype(BF16)
            p_buf[g, c] = p.astype(BF16)
            ds_buf[g, c] = ds
            total = total + dot_tn(chunk_of(k_all, c, g), ds)
        total = (SCALE * total).astype(BF16)
        half = total.shape[1] // 2
        gq[2 * g * HD : (2 * g + 1) * HD, :] = total[:, :half]
        gq[(2 * g + 1) * HD : (2 * g + 2) * HD, :] = total[:, half:]

    def gq_copy(end):
        return remote(
            gq, gq_in.at[z], gq_send.at[end], gq_recv.at[z], {"seq_0": z * 0 + end * (NZ - 1)}
        )

    for end in range(2):
        @pl.when(z != end * (NZ - 1))
        def _():
            gq_copy(end).start()

    for copy in w_copies:
        copy.wait()

    def place(k):
        return k + top_edge * (NZ - 1 - 2 * k)

    def gi_copy(k):
        return remote(
            gi_send.at[k],
            gi_recv.at[1 - top_edge],
            gi_ssem.at[k],
            gi_rsem.at[1 - top_edge],
            {"seq_0": place(k), "head": goal},
        )

    def edge_step(k):
        @pl.when(is_edge)
        def _():
            if k:
                j = place(k)
                remote(
                    gq, gq_in.at[j], gq_send.at[0], gq_recv.at[j], {"seq_0": j}
                ).wait_recv()
                operand = gq_in[j]
            else:
                operand = gq[...]
            gi_send[k] = dot_nn(w_edge[...], operand).astype(BF16)
            gi_copy(k).start()

    edge_step(0)

    terms = (gk, gv)
    chains = ((0, 1, 4, 0), (1, -1, 4, 4), (0, -1, 3, 8), (1, 1, 3, 11))
    ring_sent = []

    def ring_copy(chain, hop, src):
        kv, way, hops, slot = chain
        i = slot + hop
        return remote(src, ring.at[i], ring_send.at[i], ring_recv.at[i], both[0 if way > 0 else 1])

    def terms_unit(y0):
        for g in range(GROUPS):
            cols = slice(g * HD, (g + 1) * HD)
            gk[y0, :, cols] = (SCALE * dot_nn(ds_buf[g, y0], q2[g])).astype(BF16)
            gv[y0, :, cols] = dot_nn(p_buf[g, y0], d2[g]).astype(BF16)

    def ring_start(chain):
        kv, way, hops, slot = chain
        owner = (y + NY + way * hops) % NY
        copy = ring_copy(chain, 0, terms[kv].at[owner])
        copy.start()
        ring_sent.append(copy)

    terms_unit((y + 4) % NY)
    ring_start(chains[0])
    ring_start(chains[1])
    terms_unit((y + 3) % NY)
    ring_start(chains[3])
    terms_unit((y + 5) % NY)
    ring_start(chains[2])
    for d in (2, 6, 1, 7, 0):
        terms_unit((y + d) % NY)
    gi_own[...] = dot_nn(w_own[...], gq[...])

    for hop in range(4):
        if hop < 3:
            edge_step(hop + 1)
        for chain in chains:
            kv, way, hops, slot = chain
            if hop >= hops:
                continue
            i = slot + hop
            ring_copy(chain, hop, ring.at[i]).wait_recv()
            if hop < hops - 1:
                owner = (y + NY + way * (hops - 1 - hop)) % NY
                ring[i] = (ring[i].astype(F32) + terms[kv][owner].astype(F32)).astype(BF16)
                copy = ring_copy(chain, hop + 1, ring.at[i])
                copy.start()
                ring_sent.append(copy)
    ends = ((3, 10), (13, 7))
    line_copies = []
    for kv in range(2):
        a, b = ends[kv]
        mine[kv] = (
            (ring[a].astype(F32) + ring[b].astype(F32) + terms[kv][y].astype(F32))
            .astype(BF16)
            .reshape(mine.shape[1:])
        )
        for i, m in enumerate(mates):
            copy = remote(
                mine.at[kv, m], line.at[kv, i], line_send.at[kv, i], line_recv.at[kv, i], {"seq_0": m}
            )
            copy.start()
            line_copies.append(copy)
    for copy in line_copies:
        copy.wait_recv()
    for kv, out in enumerate((gk_out, gv_out)):
        out[...] = (
            mine[kv, z].astype(F32)
            + line[kv, 0].astype(F32)
            + line[kv, 1].astype(F32)
            + line[kv, 2].astype(F32)
        ).astype(BF16)
    for i in range(2):
        remote(
            gi_send.at[i], gi_recv.at[i], gi_ssem.at[i], gi_rsem.at[i], {"seq_1": right}
        ).wait_recv()
    gi_out[...] = (gi_own[...] + gi_recv[0].astype(F32) + gi_recv[1].astype(F32)).astype(BF16)

    for copy in sent + ring_sent + line_copies:
        copy.wait_send()
    shift.wait_send()
    for end in range(2):
        @pl.when(z != end * (NZ - 1))
        def _():
            gq_copy(end).wait_send()

    @pl.when(is_edge)
    def _():
        for k in range(NZ):
            gi_copy(k).wait_send()


def tick(span, prefix, q, d, k, v, w):
    rows, width = q.shape
    size, kv_width = k.shape
    features = w.shape[0] // NH
    chunk = NZ * size
    block = (NZ, size, kv_width)
    vmem = pl.BlockSpec(memory_space=VMEM)
    return pl.pallas_call(
        tick_kernel,
        out_shape=(
            jax.ShapeDtypeStruct((features, rows), BF16),
            jax.ShapeDtypeStruct(k.shape, BF16),
            jax.ShapeDtypeStruct(v.shape, BF16),
        ),
        in_specs=[pl.BlockSpec(memory_space=SMEM)] * 2
        + [vmem] * 4
        + [pl.BlockSpec(memory_space=pl.ANY)],
        out_specs=(vmem,) * 3,
        scratch_shapes=[
            VMEM((NY,) + block, BF16),
            VMEM((NY,) + block, BF16),
            VMEM((rows, width), BF16),
            VMEM((GROUPS, 2 * rows, HD), BF16),
            VMEM((GROUPS, 2 * rows, HD), BF16),
            VMEM((features, width), BF16),
            VMEM((features, width), BF16),
            VMEM((GROUPS, NY, chunk, 2 * rows), F32),
            VMEM((GROUPS, NY, chunk, 2 * rows), F32),
            VMEM((3, GROUPS, NY, 1, 2 * rows), F32),
            VMEM((GROUPS, NY, chunk, 2 * rows), BF16),
            VMEM((GROUPS, NY, chunk, 2 * rows), BF16),
            VMEM((NY, chunk, kv_width), BF16),
            VMEM((NY, chunk, kv_width), BF16),
            VMEM((width, rows), BF16),
            VMEM((NZ, width, rows), BF16),
            VMEM((NZ, features, rows), BF16),
            VMEM((2, features, rows), BF16),
            VMEM((features, rows), F32),
            VMEM((14, chunk, kv_width), BF16),
            VMEM((2,) + block, BF16),
            VMEM((2, 3, size, kv_width), BF16),
            DMA((124,)),
            DMA((2, NY, NZ)),
            DMA((2, NY, NZ)),
            DMA((4,)),
            DMA((2,)),
            DMA((NZ,)),
            DMA((NZ,)),
            DMA((2,)),
            DMA((14,)),
            DMA((14,)),
            DMA((2, 3)),
            DMA((2, 3)),
        ],
        compiler_params=pltpu.CompilerParams(
            collective_id=0, has_side_effects=True, vmem_limit_bytes=60 * 1024 * 1024
        ),
        name="tick",
    )(span, prefix, q, d, k, v, w)


def hand_on_kernel(*refs):
    for src, dst in zip(refs[:3], refs[3:]):
        dst[...] = src[...]


def hand_on(*arrays):
    vmem = pl.BlockSpec(memory_space=VMEM)
    return pl.pallas_call(
        hand_on_kernel,
        out_shape=tuple(jax.ShapeDtypeStruct(a.shape, a.dtype) for a in arrays),
        in_specs=[vmem] * 3,
        out_specs=(vmem,) * 3,
        name="hand_on",
    )(*arrays)


def on_device(queries, grad_out, keys, values, proj_query, section_span, span_prefix):
    outs = tick(
        section_span, span_prefix, queries[0], grad_out[0], keys[0], values[0], proj_query[0]
    )
    return tuple(a[None] for a in hand_on(*outs))


def solution(mesh):
    split = Mesh(
        mesh.devices.reshape(mesh.shape["section"], NZ, NY, mesh.shape["head"]),
        ("section", "seq_0", "seq_1", "head"),
    )
    in_specs = (
        P("section", SEQ, "head"),
        P("section", SEQ, "head"),
        P("section", SEQ, "head"),
        P("section", SEQ, "head"),
        P("section", None, "head"),
        P(),
        P(),
    )
    out_specs = (P("section", "head", SEQ), P("section", SEQ, "head"), P("section", SEQ, "head"))
    return jax.shard_map(
        on_device, mesh=split, in_specs=in_specs, out_specs=out_specs, check_vma=False
    )
```

```python
import functools
import math

import jax
import jax.numpy as jnp
from jax import lax
from jax.experimental import pallas as pl
from jax.experimental.pallas import tpu as pltpu
from jax.sharding import Mesh
from jax.sharding import PartitionSpec as P

HD = 128
SEQ = ("seq_0", "seq_1")
NZ = 4
NY = 8
NS = 8
NH = 3
GROUPS = 3
SCALE = 168.0 ** (-0.5)
SCALE_LOG2 = SCALE * math.log2(math.e)
LEAD = 16
VMEM = pltpu.VMEM
SMEM = pltpu.SMEM
DMA = pltpu.SemaphoreType.DMA
BF16 = jnp.bfloat16
F32 = jnp.float32


def column_mates(z):
    return (z + 1 - 2 * (z % 2), (z + 2) % NZ, NZ - 1 - z)


def remote(src, dst, send, recv, target):
    return pltpu.make_async_remote_copy(
        src_ref=src,
        dst_ref=dst,
        send_sem=send,
        recv_sem=recv,
        device_id=target,
        device_id_type=pl.DeviceIdType.MESH,
    )


def dot_nt(a, b):
    return lax.dot_general(a, b, (((1,), (1,)), ((), ())), preferred_element_type=F32)


def dot_nn(a, b):
    return lax.dot_general(a, b, (((1,), (0,)), ((), ())), preferred_element_type=F32)


def dot_tn(a, b):
    return lax.dot_general(a, b, (((0,), (0,)), ((), ())), preferred_element_type=F32)


def by_eight(x):
    return x.reshape(x.shape[0] // 8, 8, x.shape[1])


def flat(x):
    return x.reshape(x.shape[0] * x.shape[1], x.shape[2])


def tick_kernel(
    span_ref, prefix_ref, q_hbm, d_ref, k_ref, v_ref, w_ref,
    gi_out, gk_out, gv_out,
    q_ref, gi_fin, gkv_fin, k_all, v_all, d_new, q2, d2, w_own, w_edge,
    e_buf, dp_buf, stats, ds_buf, p_buf, gk, gv,
    gq, gq_in, gi_send, gi_recv, gi_own, ring, mine, line,
    send, recv_a, recv_b, misc, gq_send, gq_recv, gi_ssem, gi_rsem,
    ring_send, ring_recv, line_send, line_recv, in_sem, out_sem,
):
    z = lax.axis_index("seq_0")
    y = lax.axis_index("seq_1")
    h = lax.axis_index("head")
    s = lax.axis_index("section")
    right, left = (y + 1) % NY, (y + NY - 1) % NY
    mates = column_mates(z)
    lower, upper = (s + NS - 1) % NS, (s + 1) % NS
    before, after = (h + NH - 1) % NH, (h + 1) % NH
    top_edge = z // (NZ - 1)
    is_edge = (z % (NZ - 1)) == 0
    goal = (h + NH - 1 + 2 * top_edge) % NH

    barrier = pltpu.get_barrier_semaphore()

    def greet(target):
        pl.semaphore_signal(
            barrier, inc=1, device_id=target, device_id_type=pl.DeviceIdType.MESH
        )

    for target in (
        [{"seq_1": right}, {"seq_1": left}]
        + [{"seq_0": m} for m in mates]
        + [{"section": lower}, {"section": upper}]
        + [{"seq_0": z * 0 + NZ - 1, "head": before}, {"seq_0": z * 0, "head": after}]
    ):
        greet(target)

    @pl.when(is_edge)
    def _():
        for j in range(NZ):
            greet({"seq_0": z * 0 + j, "head": goal})

    own = (k_ref, v_ref)
    full = (k_all, v_all)
    in_copies = [pltpu.make_async_copy(own[kv], full[kv].at[y, z], in_sem.at[kv]) for kv in range(2)]
    in_copies.append(pltpu.make_async_copy(q_hbm, q_ref, in_sem.at[2]))
    for copy in in_copies:
        copy.start()
    pl.semaphore_wait(barrier, 9 + 4 * jnp.where(is_edge, 1, 0))

    size = k_ref.shape[0]
    rows_of = (pl.ds(0, LEAD), pl.ds(LEAD, size - LEAD))
    recv = (recv_a, recv_b)
    sent = []

    def part(kv, cls, z0, y0):
        return full[kv].at[y0, z0, rows_of[cls]]

    def push(src, kv, cls, z0, y0, target):
        copy = remote(
            src, part(kv, cls, z0, y0), send.at[len(sent)], recv[cls].at[kv, y0, z0], target
        )
        copy.start()
        sent.append(copy)

    def arrived(kv, cls, z0, y0):
        block = part(kv, cls, z0, y0)
        remote(block, block, send.at[0], recv[cls].at[kv, y0, z0], {"seq_1": right}).wait_recv()

    both = ({"seq_1": right}, {"seq_1": left})
    for kv in range(2):
        for target in both:
            push(own[kv].at[rows_of[0]], kv, 0, z, y, target)
    for m in mates:
        for kv in range(2):
            push(own[kv].at[rows_of[1]], kv, 1, z, y, {"seq_0": m})
    for kv in range(2):
        for target in both:
            push(own[kv].at[rows_of[1]], kv, 1, z, y, target)
    for m in mates:
        for kv in range(2):
            push(own[kv].at[rows_of[0]], kv, 0, z, y, {"seq_0": m})
    shift = remote(d_ref, d_new, misc.at[0], misc.at[1], {"section": lower})
    shift.start()
    w_size = w_own.shape[0]
    w_copies = [
        pltpu.make_async_copy(
            w_ref.at[pl.ds(pl.multiple_of(at * w_size, w_size), w_size), :], buf, misc.at[2 + i]
        )
        for i, (at, buf) in enumerate(((h, w_own), (goal, w_edge)))
    ]
    for copy in w_copies:
        copy.start()
    for copy in in_copies:
        copy.wait()

    length = prefix_ref[span_ref[s]]

    def halves(ref, g):
        return jnp.concatenate(
            [ref[:, 2 * g * HD : (2 * g + 1) * HD], ref[:, (2 * g + 1) * HD : (2 * g + 2) * HD]],
            axis=0,
        )

    for g in range(GROUPS):
        q2[g] = halves(q_ref, g)

    def chunk_of(ref, y0, g):
        return flat(ref[y0, :, :, g * HD : (g + 1) * HD])

    def scores_unit(y0, g):
        sc = dot_nt(chunk_of(k_all, y0, g), q2[g])
        dp = dot_nt(chunk_of(v_all, y0, g), d2[g])
        n = sc.shape[0] // 2
        i = lax.broadcasted_iota(jnp.int32, (n, sc.shape[1]), 0)
        t = i + jnp.where(i >= size, (NY - 1) * size, 0)
        live = t < length - 2 * NY * size - y0 * size
        sc = jnp.concatenate([sc[:n], jnp.where(live, sc[n:], F32(-1e30))], axis=0)
        m = by_eight(sc).max(axis=0).max(axis=0, keepdims=True)
        e = jnp.exp2((sc - m) * SCALE_LOG2)
        e_buf[g, y0] = e
        dp_buf[g, y0] = dp
        stats[0, g, y0] = m
        stats[1, g, y0] = by_eight(e).sum(axis=0).sum(axis=0, keepdims=True)
        stats[2, g, y0] = by_eight(e * dp).sum(axis=0).sum(axis=0, keepdims=True)

    reach = ((4, 3), (3, 4))

    def hop_rows(hop):
        return (y + NY - hop) % NY, (y + hop) % NY

    def lead_hop(hop):
        for kv in range(2):
            for way, y0 in enumerate(hop_rows(hop)):
                if hop <= reach[kv][way]:
                    arrived(kv, 0, z, y0)
                    if hop < reach[kv][way]:
                        push(part(kv, 0, z, y0), kv, 0, z, y0, both[way])
                    for m in mates:
                        push(part(kv, 0, z, y0), kv, 0, z, y0, {"seq_0": m})

    def bulk_hop(hop, m):
        for kv in range(2):
            for way, y0 in enumerate(hop_rows(hop)):
                if hop <= reach[kv][way]:
                    arrived(kv, 1, m, y0)
                    if hop < reach[kv][way]:
                        push(part(kv, 1, m, y0), kv, 1, m, y0, both[way])

    def column(m):
        for kv in range(2):
            arrived(kv, 1, m, y)
            for target in both:
                push(part(kv, 1, m, y), kv, 1, m, y, target)

    def units_of(rows):
        for y0 in rows:
            for kv in range(2):
                for m in mates:
                    arrived(kv, 0, m, y0)
        return [(y0, g) for y0 in rows for g in range(GROUPS)]

    for i, m in enumerate(mates):
        lead_hop(i + 1)
        bulk_hop(i + 1, z)
        column(m)
    shift.wait_recv()
    for g in range(GROUPS):
        d2[g] = halves(d_new, g)
    lead_hop(4)
    bulk_hop(4, z)
    todo = [y]
    for hop in range(1, 5):
        bulk_hop(hop, mates[0])
        units = units_of(todo)
        for m in mates[1:] + (None,):
            for unit in units[:2]:
                scores_unit(*unit)
            units = units[2:]
            if m is not None:
                bulk_hop(hop, m)
        todo = hop_rows(hop) if hop < 4 else hop_rows(hop)[:1]
    for unit in units_of(todo):
        scores_unit(*unit)

    for g in range(GROUPS):
        m_c = [stats[0, g, c] for c in range(NY)]
        top = functools.reduce(jnp.maximum, m_c)
        f_c = [jnp.exp2((m - top) * SCALE_LOG2) for m in m_c]
        inv = 1.0 / sum(f * stats[1, g, c] for c, f in enumerate(f_c))
        delta = sum(f * stats[2, g, c] for c, f in enumerate(f_c)) * inv
        total = jnp.zeros((HD, q2.shape[1]), F32)
        for c in range(NY):
            p = e_buf[g, c] * (f_c[c] * inv)
            ds = (p * (dp_buf[g, c] - delta)).astype(BF16)
            p_buf[g, c] = p.astype(BF16)
            ds_buf[g, c] = ds
            total = total + dot_tn(chunk_of(k_all, c, g), ds)
        total = (SCALE * total).astype(BF16)
        half = total.shape[1] // 2
        gq[2 * g * HD : (2 * g + 1) * HD, :] = total[:, :half]
        gq[(2 * g + 1) * HD : (2 * g + 2) * HD, :] = total[:, half:]

    def gq_copy(end):
        return remote(
            gq, gq_in.at[z], gq_send.at[end], gq_recv.at[z], {"seq_0": z * 0 + end * (NZ - 1)}
        )

    for end in range(2):
        @pl.when(z != end * (NZ - 1))
        def _():
            gq_copy(end).start()

    for copy in w_copies:
        copy.wait()

    def place(k):
        return k + top_edge * (NZ - 1 - 2 * k)

    def gi_copy(k):
        return remote(
            gi_send.at[k],
            gi_recv.at[1 - top_edge],
            gi_ssem.at[k],
            gi_rsem.at[1 - top_edge],
            {"seq_0": place(k), "head": goal},
        )

    def edge_step(k):
        @pl.when(is_edge)
        def _():
            if k:
                j = place(k)
                remote(
                    gq, gq_in.at[j], gq_send.at[0], gq_recv.at[j], {"seq_0": j}
                ).wait_recv()
                operand = gq_in[j]
            else:
                operand = gq[...]
            gi_send[k] = dot_nn(w_edge[...], operand).astype(BF16)
            gi_copy(k).start()

    edge_step(0)

    terms = (gk, gv)
    chains = ((0, 1, 4, 0), (1, -1, 4, 4), (0, -1, 3, 8), (1, 1, 3, 11))
    ring_sent = []

    def ring_copy(chain, hop, src):
        kv, way, hops, slot = chain
        i = slot + hop
        return remote(src, ring.at[i], ring_send.at[i], ring_recv.at[i], both[0 if way > 0 else 1])

    def terms_unit(y0):
        for g in range(GROUPS):
            cols = slice(g * HD, (g + 1) * HD)
            gk[y0, :, cols] = (SCALE * dot_nn(ds_buf[g, y0], q2[g])).astype(BF16)
            gv[y0, :, cols] = dot_nn(p_buf[g, y0], d2[g]).astype(BF16)

    def ring_start(chain):
        kv, way, hops, slot = chain
        owner = (y + NY + way * hops) % NY
        copy = ring_copy(chain, 0, terms[kv].at[owner])
        copy.start()
        ring_sent.append(copy)

    terms_unit((y + 4) % NY)
    ring_start(chains[0])
    ring_start(chains[1])
    terms_unit((y + 3) % NY)
    ring_start(chains[3])
    terms_unit((y + 5) % NY)
    ring_start(chains[2])
    for d in (2, 6, 1, 7, 0):
        terms_unit((y + d) % NY)
    gi_own[...] = dot_nn(w_own[...], gq[...])

    for hop in range(4):
        for at, chain in enumerate(chains):
            if at == 2 and hop < 3:
                edge_step(hop + 1)
            kv, way, hops, slot = chain
            if hop >= hops:
                continue
            i = slot + hop
            ring_copy(chain, hop, ring.at[i]).wait_recv()
            if hop < hops - 1:
                owner = (y + NY + way * (hops - 1 - hop)) % NY
                ring[i] = (ring[i].astype(F32) + terms[kv][owner].astype(F32)).astype(BF16)
                copy = ring_copy(chain, hop + 1, ring.at[i])
                copy.start()
                ring_sent.append(copy)
    ends = ((3, 10), (13, 7))
    line_copies = []
    for kv in range(2):
        a, b = ends[kv]
        mine[kv] = (
            (ring[a].astype(F32) + ring[b].astype(F32) + terms[kv][y].astype(F32))
            .astype(BF16)
            .reshape(mine.shape[1:])
        )
        for i, m in enumerate(mates):
            copy = remote(
                mine.at[kv, m], line.at[kv, i], line_send.at[kv, i], line_recv.at[kv, i], {"seq_0": m}
            )
            copy.start()
            line_copies.append(copy)
    for copy in line_copies:
        copy.wait_recv()
    out_copies = []
    for kv, out in enumerate((gk_out, gv_out)):
        gkv_fin[kv] = (
            mine[kv, z].astype(F32)
            + line[kv, 0].astype(F32)
            + line[kv, 1].astype(F32)
            + line[kv, 2].astype(F32)
        ).astype(BF16)
        out_copies.append(pltpu.make_async_copy(gkv_fin.at[kv], out, out_sem.at[kv]))
        out_copies[-1].start()
    for i in range(2):
        remote(
            gi_send.at[i], gi_recv.at[i], gi_ssem.at[i], gi_rsem.at[i], {"seq_1": right}
        ).wait_recv()
    gi_fin[...] = (gi_own[...] + gi_recv[0].astype(F32) + gi_recv[1].astype(F32)).astype(BF16)
    out_copies.append(pltpu.make_async_copy(gi_fin, gi_out, out_sem.at[2]))
    out_copies[-1].start()

    for copy in sent + ring_sent + line_copies:
        copy.wait_send()
    shift.wait_send()
    for end in range(2):
        @pl.when(z != end * (NZ - 1))
        def _():
            gq_copy(end).wait_send()

    @pl.when(is_edge)
    def _():
        for k in range(NZ):
            gi_copy(k).wait_send()

    for copy in out_copies:
        copy.wait()


def tick(span, prefix, q, d, k, v, w):
    rows, width = q.shape
    size, kv_width = k.shape
    features = w.shape[0] // NH
    chunk = NZ * size
    block = (NZ, size, kv_width)
    return pl.pallas_call(
        tick_kernel,
        out_shape=(
            jax.ShapeDtypeStruct((features, rows), BF16),
            jax.ShapeDtypeStruct(k.shape, BF16),
            jax.ShapeDtypeStruct(v.shape, BF16),
        ),
        in_specs=[pl.BlockSpec(memory_space=SMEM)] * 2
        + [pl.BlockSpec(memory_space=pl.ANY)] * 5,
        out_specs=(pl.BlockSpec(memory_space=pl.ANY),) * 3,
        scratch_shapes=[
            VMEM(q.shape, BF16),
            VMEM((features, rows), BF16),
            VMEM((2,) + k.shape, BF16),
            VMEM((NY,) + block, BF16),
            VMEM((NY,) + block, BF16),
            VMEM((rows, width), BF16),
            VMEM((GROUPS, 2 * rows, HD), BF16),
            VMEM((GROUPS, 2 * rows, HD), BF16),
            VMEM((features, width), BF16),
            VMEM((features, width), BF16),
            VMEM((GROUPS, NY, chunk, 2 * rows), F32),
            VMEM((GROUPS, NY, chunk, 2 * rows), F32),
            VMEM((3, GROUPS, NY, 1, 2 * rows), F32),
            VMEM((GROUPS, NY, chunk, 2 * rows), BF16),
            VMEM((GROUPS, NY, chunk, 2 * rows), BF16),
            VMEM((NY, chunk, kv_width), BF16),
            VMEM((NY, chunk, kv_width), BF16),
            VMEM((width, rows), BF16),
            VMEM((NZ, width, rows), BF16),
            VMEM((NZ, features, rows), BF16),
            VMEM((2, features, rows), BF16),
            VMEM((features, rows), F32),
            VMEM((14, chunk, kv_width), BF16),
            VMEM((2,) + block, BF16),
            VMEM((2, 3, size, kv_width), BF16),
            DMA((124,)),
            DMA((2, NY, NZ)),
            DMA((2, NY, NZ)),
            DMA((4,)),
            DMA((2,)),
            DMA((NZ,)),
            DMA((NZ,)),
            DMA((2,)),
            DMA((14,)),
            DMA((14,)),
            DMA((2, 3)),
            DMA((2, 3)),
            DMA((3,)),
            DMA((3,)),
        ],
        compiler_params=pltpu.CompilerParams(
            collective_id=0, has_side_effects=True, vmem_limit_bytes=60 * 1024 * 1024
        ),
        name="tick",
    )(span, prefix, q, d, k, v, w)


def hand_on_kernel(*refs):
    for src, dst in zip(refs[:3], refs[3:]):
        dst[...] = src[...]


def hand_on(*arrays):
    vmem = pl.BlockSpec(memory_space=VMEM)
    return pl.pallas_call(
        hand_on_kernel,
        out_shape=tuple(jax.ShapeDtypeStruct(a.shape, a.dtype) for a in arrays),
        in_specs=[vmem] * 3,
        out_specs=(vmem,) * 3,
        name="hand_on",
    )(*arrays)


def on_device(queries, grad_out, keys, values, proj_query, section_span, span_prefix):
    outs = tick(
        section_span, span_prefix, queries[0], grad_out[0], keys[0], values[0], proj_query[0]
    )
    return tuple(a[None] for a in hand_on(*outs))


def solution(mesh):
    split = Mesh(
        mesh.devices.reshape(mesh.shape["section"], NZ, NY, mesh.shape["head"]),
        ("section", "seq_0", "seq_1", "head"),
    )
    in_specs = (
        P("section", SEQ, "head"),
        P("section", SEQ, "head"),
        P("section", SEQ, "head"),
        P("section", SEQ, "head"),
        P("section", None, "head"),
        P(),
        P(),
    )
    out_specs = (P("section", "head", SEQ), P("section", SEQ, "head"), P("section", SEQ, "head"))
    return jax.shard_map(
        on_device, mesh=split, in_specs=in_specs, out_specs=out_specs, check_vma=False
    )
```

```python
import functools
import math

import jax
import jax.numpy as jnp
from jax import lax
from jax.experimental import pallas as pl
from jax.experimental.pallas import tpu as pltpu
from jax.sharding import Mesh
from jax.sharding import PartitionSpec as P

HD = 128
SEQ = ("seq_0", "seq_1")
NZ = 4
NY = 8
NS = 8
NH = 3
GROUPS = 3
SCALE = 168.0 ** (-0.5)
SCALE_LOG2 = SCALE * math.log2(math.e)
LEAD = 16
VMEM = pltpu.VMEM
SMEM = pltpu.SMEM
DMA = pltpu.SemaphoreType.DMA
BF16 = jnp.bfloat16
F32 = jnp.float32


def column_mates(z):
    return (z + 1 - 2 * (z % 2), (z + 2) % NZ, NZ - 1 - z)


def remote(src, dst, send, recv, target):
    return pltpu.make_async_remote_copy(
        src_ref=src,
        dst_ref=dst,
        send_sem=send,
        recv_sem=recv,
        device_id=target,
        device_id_type=pl.DeviceIdType.MESH,
    )


def dot_nt(a, b):
    return lax.dot_general(a, b, (((1,), (1,)), ((), ())), preferred_element_type=F32)


def dot_nn(a, b):
    return lax.dot_general(a, b, (((1,), (0,)), ((), ())), preferred_element_type=F32)


def dot_tn(a, b):
    return lax.dot_general(a, b, (((0,), (0,)), ((), ())), preferred_element_type=F32)


def by_eight(x):
    return x.reshape(x.shape[0] // 8, 8, x.shape[1])


def flat(x):
    return x.reshape(x.shape[0] * x.shape[1], x.shape[2])


def tick_kernel(
    span_ref, prefix_ref, q_hbm, d_ref, k_ref, v_ref, w_ref,
    gi_out, gk_out, gv_out,
    q_ref, gi_fin, gkv_fin, k_all, v_all, d_new, q2, d2, w_own, w_edge,
    e_buf, dp_buf, stats, ds_buf, p_buf, gk, gv,
    gq, gq_in, gi_send, gi_recv, gi_own, ring, mine, line,
    send, recv_a, recv_b, misc, gq_send, gq_recv, gi_ssem, gi_rsem,
    ring_send, ring_recv, line_send, line_recv, in_sem, out_sem,
):
    z = lax.axis_index("seq_0")
    y = lax.axis_index("seq_1")
    h = lax.axis_index("head")
    s = lax.axis_index("section")
    right, left = (y + 1) % NY, (y + NY - 1) % NY
    mates = column_mates(z)
    lower, upper = (s + NS - 1) % NS, (s + 1) % NS
    before, after = (h + NH - 1) % NH, (h + 1) % NH
    top_edge = z // (NZ - 1)
    is_edge = (z % (NZ - 1)) == 0
    side = z // 2
    goal = (h + NH - 1 + 2 * side) % NH

    def place(distance):
        return distance + top_edge * (NZ - 1 - 2 * distance)

    own_goal = {"seq_0": z, "head": goal}
    far_goals = [{"seq_0": place(distance), "head": goal} for distance in (2, 3)]

    barrier = pltpu.get_barrier_semaphore()

    def greet(target):
        pl.semaphore_signal(
            barrier, inc=1, device_id=target, device_id_type=pl.DeviceIdType.MESH
        )

    for target in (
        [{"seq_1": right}, {"seq_1": left}]
        + [{"seq_0": m} for m in mates]
        + [{"section": lower}, {"section": upper}]
        + [
            {"seq_0": z * side + (NZ - 1) * (1 - side), "head": before},
            {"seq_0": z * (1 - side), "head": after},
            own_goal,
        ]
    ):
        greet(target)

    @pl.when(is_edge)
    def _():
        for target in far_goals:
            greet(target)

    own = (k_ref, v_ref)
    full = (k_all, v_all)
    in_copies = [pltpu.make_async_copy(own[kv], full[kv].at[y, z], in_sem.at[kv]) for kv in range(2)]
    in_copies.append(pltpu.make_async_copy(q_hbm, q_ref, in_sem.at[2]))
    for copy in in_copies:
        copy.start()
    pl.semaphore_wait(barrier, 10 + 2 * jnp.where(is_edge, 1, 0))

    size = k_ref.shape[0]
    rows_of = (pl.ds(0, LEAD), pl.ds(LEAD, size - LEAD))
    recv = (recv_a, recv_b)
    sent = []

    def part(kv, cls, z0, y0):
        return full[kv].at[y0, z0, rows_of[cls]]

    def push(src, kv, cls, z0, y0, target):
        copy = remote(
            src, part(kv, cls, z0, y0), send.at[0], recv[cls].at[kv, y0, z0], target
        )
        copy.start()
        sent.append(LEAD if cls == 0 else size - LEAD)

    def arrived(kv, cls, z0, y0):
        block = part(kv, cls, z0, y0)
        remote(block, block, send.at[0], recv[cls].at[kv, y0, z0], {"seq_1": right}).wait_recv()

    both = ({"seq_1": right}, {"seq_1": left})
    for kv in range(2):
        for target in both:
            push(own[kv].at[rows_of[0]], kv, 0, z, y, target)
    for m in mates:
        for kv in range(2):
            push(own[kv].at[rows_of[1]], kv, 1, z, y, {"seq_0": m})
    for kv in range(2):
        for target in both:
            push(own[kv].at[rows_of[1]], kv, 1, z, y, target)
    for m in mates:
        for kv in range(2):
            push(own[kv].at[rows_of[0]], kv, 0, z, y, {"seq_0": m})
    shift = remote(d_ref, d_new, misc.at[0], misc.at[1], {"section": lower})
    shift.start()
    w_size = w_own.shape[0]
    w_copies = [
        pltpu.make_async_copy(
            w_ref.at[pl.ds(pl.multiple_of(at * w_size, w_size), w_size), :], buf, misc.at[2 + i]
        )
        for i, (at, buf) in enumerate(((h, w_own), (goal, w_edge)))
    ]
    for copy in w_copies:
        copy.start()
    for copy in in_copies:
        copy.wait()

    length = prefix_ref[span_ref[s]]

    def halves(ref, g):
        return jnp.concatenate(
            [ref[:, 2 * g * HD : (2 * g + 1) * HD], ref[:, (2 * g + 1) * HD : (2 * g + 2) * HD]],
            axis=0,
        )

    for g in range(GROUPS):
        q2[g] = halves(q_ref, g)

    def chunk_of(ref, y0, g):
        return flat(ref[y0, :, :, g * HD : (g + 1) * HD])

    def scores_unit(y0, g):
        sc = dot_nt(chunk_of(k_all, y0, g), q2[g])
        dp = dot_nt(chunk_of(v_all, y0, g), d2[g])
        n = sc.shape[0] // 2
        i = lax.broadcasted_iota(jnp.int32, (n, sc.shape[1]), 0)
        t = i + jnp.where(i >= size, (NY - 1) * size, 0)
        live = t < length - 2 * NY * size - y0 * size
        sc = jnp.concatenate([sc[:n], jnp.where(live, sc[n:], F32(-1e30))], axis=0)
        m = by_eight(sc).max(axis=0).max(axis=0, keepdims=True)
        e = jnp.exp2((sc - m) * SCALE_LOG2)
        e_buf[g, y0] = e
        dp_buf[g, y0] = dp
        stats[0, g, y0] = m
        stats[1, g, y0] = by_eight(e).sum(axis=0).sum(axis=0, keepdims=True)
        stats[2, g, y0] = by_eight(e * dp).sum(axis=0).sum(axis=0, keepdims=True)

    reach = ((4, 3), (3, 4))

    def hop_rows(hop):
        return (y + NY - hop) % NY, (y + hop) % NY

    def lead_hop(hop):
        for kv in range(2):
            for way, y0 in enumerate(hop_rows(hop)):
                if hop <= reach[kv][way]:
                    arrived(kv, 0, z, y0)
                    if hop < reach[kv][way]:
                        push(part(kv, 0, z, y0), kv, 0, z, y0, both[way])
                    for m in mates:
                        push(part(kv, 0, z, y0), kv, 0, z, y0, {"seq_0": m})

    def bulk_hop(hop, m):
        for kv in range(2):
            for way, y0 in enumerate(hop_rows(hop)):
                if hop <= reach[kv][way]:
                    arrived(kv, 1, m, y0)
                    if hop < reach[kv][way]:
                        push(part(kv, 1, m, y0), kv, 1, m, y0, both[way])

    def column(m):
        for kv in range(2):
            arrived(kv, 1, m, y)
            for target in both:
                push(part(kv, 1, m, y), kv, 1, m, y, target)

    def units_of(rows):
        for y0 in rows:
            for kv in range(2):
                for m in mates:
                    arrived(kv, 0, m, y0)
        return [(y0, g) for y0 in rows for g in range(GROUPS)]

    for i, m in enumerate(mates):
        lead_hop(i + 1)
        bulk_hop(i + 1, z)
        column(m)
    shift.wait_recv()
    for g in range(GROUPS):
        d2[g] = halves(d_new, g)
    lead_hop(4)
    bulk_hop(4, z)
    todo = [y]
    for hop in range(1, 5):
        bulk_hop(hop, mates[0])
        units = units_of(todo)
        for m in mates[1:] + (None,):
            for unit in units[:2]:
                scores_unit(*unit)
            units = units[2:]
            if m is not None:
                bulk_hop(hop, m)
        todo = hop_rows(hop) if hop < 4 else hop_rows(hop)[:1]
    for unit in units_of(todo):
        scores_unit(*unit)

    for g in range(GROUPS):
        m_c = [stats[0, g, c] for c in range(NY)]
        top = functools.reduce(jnp.maximum, m_c)
        f_c = [jnp.exp2((m - top) * SCALE_LOG2) for m in m_c]
        inv = 1.0 / sum(f * stats[1, g, c] for c, f in enumerate(f_c))
        delta = sum(f * stats[2, g, c] for c, f in enumerate(f_c)) * inv
        total = jnp.zeros((HD, q2.shape[1]), F32)
        for c in range(NY):
            p = e_buf[g, c] * (f_c[c] * inv)
            ds = (p * (dp_buf[g, c] - delta)).astype(BF16)
            p_buf[g, c] = p.astype(BF16)
            ds_buf[g, c] = ds
            total = total + dot_tn(chunk_of(k_all, c, g), ds)
        total = (SCALE * total).astype(BF16)
        half = total.shape[1] // 2
        gq[2 * g * HD : (2 * g + 1) * HD, :] = total[:, :half]
        gq[(2 * g + 1) * HD : (2 * g + 2) * HD, :] = total[:, half:]

    def gq_copy(end):
        return remote(
            gq, gq_in.at[z], gq_send.at[end], gq_recv.at[z], {"seq_0": z * 0 + end * (NZ - 1)}
        )

    def gq_leaves(distance):
        for end in range(2):
            @pl.when(z == end * (NZ - 1) + distance * (1 - 2 * end))
            def _():
                gq_copy(end).start()

    gq_leaves(2)
    for copy in w_copies:
        copy.wait()

    def gi_copy(k):
        return remote(
            gi_send.at[k],
            gi_recv.at[1 - side],
            gi_ssem.at[k],
            gi_rsem.at[1 - side],
            far_goals[k - 1] if k else own_goal,
        )

    gi_send[0] = dot_nn(w_edge[...], gq[...]).astype(BF16)
    gi_copy(0).start()

    def edge_step(k):
        @pl.when(is_edge)
        def _():
            j = place(k + 1)
            remote(gq, gq_in.at[j], gq_send.at[0], gq_recv.at[j], {"seq_0": j}).wait_recv()
            gi_send[k] = dot_nn(w_edge[...], gq_in[j]).astype(BF16)
            gi_copy(k).start()

    terms = (gk, gv)
    chains = ((0, 1, 4, 0), (1, -1, 4, 4), (0, -1, 3, 8), (1, 1, 3, 11))
    ring_sent = []

    def ring_copy(chain, hop, src):
        kv, way, hops, slot = chain
        i = slot + hop
        return remote(src, ring.at[i], ring_send.at[i], ring_recv.at[i], both[0 if way > 0 else 1])

    def terms_unit(y0):
        for g in range(GROUPS):
            cols = slice(g * HD, (g + 1) * HD)
            gk[y0, :, cols] = (SCALE * dot_nn(ds_buf[g, y0], q2[g])).astype(BF16)
            gv[y0, :, cols] = dot_nn(p_buf[g, y0], d2[g]).astype(BF16)

    def ring_start(chain):
        kv, way, hops, slot = chain
        owner = (y + NY + way * hops) % NY
        copy = ring_copy(chain, 0, terms[kv].at[owner])
        copy.start()
        ring_sent.append(copy)

    terms_unit((y + 4) % NY)
    ring_start(chains[0])
    ring_start(chains[1])
    terms_unit((y + 3) % NY)
    ring_start(chains[3])
    terms_unit((y + 5) % NY)
    ring_start(chains[2])
    for d in (2, 6, 1, 7, 0):
        terms_unit((y + d) % NY)
    gq_leaves(3)
    gi_own[...] = dot_nn(w_own[...], gq[...])

    for hop in range(4):
        for at, chain in enumerate(chains):
            if at == 2 and hop in (1, 2):
                edge_step(hop)
            kv, way, hops, slot = chain
            if hop >= hops:
                continue
            i = slot + hop
            ring_copy(chain, hop, ring.at[i]).wait_recv()
            if hop < hops - 1:
                owner = (y + NY + way * (hops - 1 - hop)) % NY
                ring[i] = (ring[i].astype(F32) + terms[kv][owner].astype(F32)).astype(BF16)
                copy = ring_copy(chain, hop + 1, ring.at[i])
                copy.start()
                ring_sent.append(copy)
    ends = ((3, 10), (13, 7))
    line_copies = []
    for kv in range(2):
        a, b = ends[kv]
        mine[kv] = (
            (ring[a].astype(F32) + ring[b].astype(F32) + terms[kv][y].astype(F32))
            .astype(BF16)
            .reshape(mine.shape[1:])
        )
        for i, m in enumerate(mates):
            copy = remote(
                mine.at[kv, m], line.at[kv, i], line_send.at[kv, i], line_recv.at[kv, i], {"seq_0": m}
            )
            copy.start()
            line_copies.append(copy)
    for copy in line_copies:
        copy.wait_recv()
    out_copies = []
    for kv, out in enumerate((gk_out, gv_out)):
        gkv_fin[kv] = (
            mine[kv, z].astype(F32)
            + line[kv, 0].astype(F32)
            + line[kv, 1].astype(F32)
            + line[kv, 2].astype(F32)
        ).astype(BF16)
        out_copies.append(pltpu.make_async_copy(gkv_fin.at[kv], out, out_sem.at[kv]))
        out_copies[-1].start()
    for i in range(2):
        remote(
            gi_send.at[i], gi_recv.at[i], gi_ssem.at[i], gi_rsem.at[i], {"seq_1": right}
        ).wait_recv()
    gi_fin[...] = (gi_own[...] + gi_recv[0].astype(F32) + gi_recv[1].astype(F32)).astype(BF16)
    out_copies.append(pltpu.make_async_copy(gi_fin, gi_out, out_sem.at[2]))
    out_copies[-1].start()

    gather_rows = sum(n for n in sent) * k_ref.shape[1] // w_ref.shape[1]
    gather_all = w_ref.at[pl.ds(0, gather_rows), :]
    remote(gather_all, gather_all, send.at[0], misc.at[1], both[0]).wait_send()
    for copy in ring_sent + line_copies:
        copy.wait_send()
    shift.wait_send()
    for end in range(2):
        @pl.when(side != end)
        def _():
            gq_copy(end).wait_send()

    gi_copy(0).wait_send()

    @pl.when(is_edge)
    def _():
        for k in (1, 2):
            gi_copy(k).wait_send()

    for copy in out_copies:
        copy.wait()


def tick(span, prefix, q, d, k, v, w):
    rows, width = q.shape
    size, kv_width = k.shape
    features = w.shape[0] // NH
    chunk = NZ * size
    block = (NZ, size, kv_width)
    return pl.pallas_call(
        tick_kernel,
        out_shape=(
            jax.ShapeDtypeStruct((features, rows), BF16),
            jax.ShapeDtypeStruct(k.shape, BF16),
            jax.ShapeDtypeStruct(v.shape, BF16),
        ),
        in_specs=[pl.BlockSpec(memory_space=SMEM)] * 2
        + [pl.BlockSpec(memory_space=pl.ANY)] * 5,
        out_specs=(pl.BlockSpec(memory_space=pl.ANY),) * 3,
        scratch_shapes=[
            VMEM(q.shape, BF16),
            VMEM((features, rows), BF16),
            VMEM((2,) + k.shape, BF16),
            VMEM((NY,) + block, BF16),
            VMEM((NY,) + block, BF16),
            VMEM((rows, width), BF16),
            VMEM((GROUPS, 2 * rows, HD), BF16),
            VMEM((GROUPS, 2 * rows, HD), BF16),
            VMEM((features, width), BF16),
            VMEM((features, width), BF16),
            VMEM((GROUPS, NY, chunk, 2 * rows), F32),
            VMEM((GROUPS, NY, chunk, 2 * rows), F32),
            VMEM((3, GROUPS, NY, 1, 2 * rows), F32),
            VMEM((GROUPS, NY, chunk, 2 * rows), BF16),
            VMEM((GROUPS, NY, chunk, 2 * rows), BF16),
            VMEM((NY, chunk, kv_width), BF16),
            VMEM((NY, chunk, kv_width), BF16),
            VMEM((width, rows), BF16),
            VMEM((NZ, width, rows), BF16),
            VMEM((3, features, rows), BF16),
            VMEM((2, features, rows), BF16),
            VMEM((features, rows), F32),
            VMEM((14, chunk, kv_width), BF16),
            VMEM((2,) + block, BF16),
            VMEM((2, 3, size, kv_width), BF16),
            DMA((1,)),
            DMA((2, NY, NZ)),
            DMA((2, NY, NZ)),
            DMA((4,)),
            DMA((2,)),
            DMA((NZ,)),
            DMA((3,)),
            DMA((2,)),
            DMA((14,)),
            DMA((14,)),
            DMA((2, 3)),
            DMA((2, 3)),
            DMA((3,)),
            DMA((3,)),
        ],
        compiler_params=pltpu.CompilerParams(
            collective_id=0, has_side_effects=True, vmem_limit_bytes=60 * 1024 * 1024
        ),
        name="tick",
    )(span, prefix, q, d, k, v, w)


def hand_on_kernel(*refs):
    for src, dst in zip(refs[:3], refs[3:]):
        dst[...] = src[...]


def hand_on(*arrays):
    vmem = pl.BlockSpec(memory_space=VMEM)
    return pl.pallas_call(
        hand_on_kernel,
        out_shape=tuple(jax.ShapeDtypeStruct(a.shape, a.dtype) for a in arrays),
        in_specs=[vmem] * 3,
        out_specs=(vmem,) * 3,
        name="hand_on",
    )(*arrays)


def on_device(queries, grad_out, keys, values, proj_query, section_span, span_prefix):
    outs = tick(
        section_span, span_prefix, queries[0], grad_out[0], keys[0], values[0], proj_query[0]
    )
    return tuple(a[None] for a in hand_on(*outs))


def solution(mesh):
    split = Mesh(
        mesh.devices.reshape(mesh.shape["section"], NZ, NY, mesh.shape["head"]),
        ("section", "seq_0", "seq_1", "head"),
    )
    in_specs = (
        P("section", SEQ, "head"),
        P("section", SEQ, "head"),
        P("section", SEQ, "head"),
        P("section", SEQ, "head"),
        P("section", None, "head"),
        P(),
        P(),
    )
    out_specs = (P("section", "head", SEQ), P("section", SEQ, "head"), P("section", SEQ, "head"))
    return jax.shard_map(
        on_device, mesh=split, in_specs=in_specs, out_specs=out_specs, check_vma=False
    )
```

```python
import functools
import math

import jax
import jax.numpy as jnp
from jax import lax
from jax.experimental import pallas as pl
from jax.experimental.pallas import tpu as pltpu
from jax.sharding import Mesh
from jax.sharding import PartitionSpec as P

HD = 128
SEQ = ("seq_0", "seq_1")
NZ = 4
NY = 8
NS = 8
NH = 3
GROUPS = 3
SCALE = 168.0 ** (-0.5)
SCALE_LOG2 = SCALE * math.log2(math.e)
LEAD = 16
VMEM = pltpu.VMEM
SMEM = pltpu.SMEM
DMA = pltpu.SemaphoreType.DMA
BF16 = jnp.bfloat16
F32 = jnp.float32


def column_mates(z):
    return (z + 1 - 2 * (z % 2), (z + 2) % NZ, NZ - 1 - z)


def remote(src, dst, send, recv, target):
    return pltpu.make_async_remote_copy(
        src_ref=src,
        dst_ref=dst,
        send_sem=send,
        recv_sem=recv,
        device_id=target,
        device_id_type=pl.DeviceIdType.MESH,
    )


def dot_nt(a, b):
    return lax.dot_general(a, b, (((1,), (1,)), ((), ())), preferred_element_type=F32)


def dot_nn(a, b):
    return lax.dot_general(a, b, (((1,), (0,)), ((), ())), preferred_element_type=F32)


def dot_tn(a, b):
    return lax.dot_general(a, b, (((0,), (0,)), ((), ())), preferred_element_type=F32)


def by_eight(x):
    return x.reshape(x.shape[0] // 8, 8, x.shape[1])


def flat(x):
    return x.reshape(x.shape[0] * x.shape[1], x.shape[2])


def tick_kernel(
    span_ref, prefix_ref, q_hbm, d_ref, k_ref, v_ref, w_ref,
    gi_out, gk_out, gv_out,
    q_ref, gi_fin, gkv_fin, k_all, v_all, d_new, q2, d2, w_own, w_edge,
    e_buf, dp_buf, stats, ds_buf, p_buf, gk, gv,
    gq, gq_in, gi_send, gi_recv, gi_own, ring, mine, line,
    send, recv_a, recv_b, misc, gq_send, gq_recv, gi_ssem, gi_rsem,
    ring_send, ring_recv, line_send, line_recv, in_sem, out_sem,
):
    z = lax.axis_index("seq_0")
    y = lax.axis_index("seq_1")
    h = lax.axis_index("head")
    s = lax.axis_index("section")
    right, left = (y + 1) % NY, (y + NY - 1) % NY
    mates = column_mates(z)
    lower, upper = (s + NS - 1) % NS, (s + 1) % NS
    before, after = (h + NH - 1) % NH, (h + 1) % NH
    top_edge = z // (NZ - 1)
    is_edge = (z % (NZ - 1)) == 0
    side = z // 2
    goal = (h + NH - 1 + 2 * side) % NH

    def place(distance):
        return distance + top_edge * (NZ - 1 - 2 * distance)

    own_goal = {"seq_0": z, "head": goal}
    far_goals = [{"seq_0": place(distance), "head": goal} for distance in (2, 3)]

    barrier = pltpu.get_barrier_semaphore()

    def greet(target):
        pl.semaphore_signal(
            barrier, inc=1, device_id=target, device_id_type=pl.DeviceIdType.MESH
        )

    for target in (
        [{"seq_1": right}, {"seq_1": left}]
        + [{"seq_0": m} for m in mates]
        + [{"section": lower}, {"section": upper}]
        + [
            {"seq_0": z * side + (NZ - 1) * (1 - side), "head": before},
            {"seq_0": z * (1 - side), "head": after},
            own_goal,
        ]
    ):
        greet(target)

    @pl.when(is_edge)
    def _():
        for target in far_goals:
            greet(target)

    own = (k_ref, v_ref)
    full = (k_all, v_all)
    in_copies = [pltpu.make_async_copy(own[kv], full[kv].at[y, z], in_sem.at[kv]) for kv in range(2)]
    in_copies.append(pltpu.make_async_copy(q_hbm, q_ref, in_sem.at[2]))
    for copy in in_copies:
        copy.start()
    pl.semaphore_wait(barrier, 10 + 2 * jnp.where(is_edge, 1, 0))

    size = k_ref.shape[0]
    rows_of = (pl.ds(0, LEAD), pl.ds(LEAD, size - LEAD))
    recv = (recv_a, recv_b)
    sent = []

    def part(kv, cls, z0, y0):
        return full[kv].at[y0, z0, rows_of[cls]]

    def push(src, kv, cls, z0, y0, target):
        copy = remote(
            src, part(kv, cls, z0, y0), send.at[0], recv[cls].at[kv, y0, z0], target
        )
        copy.start()
        sent.append(LEAD if cls == 0 else size - LEAD)

    def arrived(kv, cls, z0, y0):
        block = part(kv, cls, z0, y0)
        remote(block, block, send.at[0], recv[cls].at[kv, y0, z0], {"seq_1": right}).wait_recv()

    both = ({"seq_1": right}, {"seq_1": left})
    for kv in range(2):
        for target in both:
            push(own[kv].at[rows_of[0]], kv, 0, z, y, target)
    for m in mates:
        for kv in range(2):
            push(own[kv].at[rows_of[1]], kv, 1, z, y, {"seq_0": m})
    for kv in range(2):
        for target in both:
            push(own[kv].at[rows_of[1]], kv, 1, z, y, target)
    for m in mates:
        for kv in range(2):
            push(own[kv].at[rows_of[0]], kv, 0, z, y, {"seq_0": m})
    shift = remote(d_ref, d_new, misc.at[0], misc.at[1], {"section": lower})
    shift.start()
    w_size = w_own.shape[0]
    w_copies = [
        pltpu.make_async_copy(
            w_ref.at[pl.ds(pl.multiple_of(at * w_size, w_size), w_size), :], buf, misc.at[2 + i]
        )
        for i, (at, buf) in enumerate(((h, w_own), (goal, w_edge)))
    ]
    for copy in w_copies:
        copy.start()
    for copy in in_copies:
        copy.wait()

    length = prefix_ref[span_ref[s]]

    def halves(ref, g):
        return jnp.concatenate(
            [ref[:, 2 * g * HD : (2 * g + 1) * HD], ref[:, (2 * g + 1) * HD : (2 * g + 2) * HD]],
            axis=0,
        )

    for g in range(GROUPS):
        q2[g] = halves(q_ref, g)

    def chunk_of(ref, y0, g):
        return flat(ref[y0, :, :, g * HD : (g + 1) * HD])

    def scores_unit(y0, g):
        sc = dot_nt(chunk_of(k_all, y0, g), q2[g])
        dp = dot_nt(chunk_of(v_all, y0, g), d2[g])
        n = sc.shape[0] // 2
        i = lax.broadcasted_iota(jnp.int32, (n, sc.shape[1]), 0)
        t = i + jnp.where(i >= size, (NY - 1) * size, 0)
        live = t < length - 2 * NY * size - y0 * size
        sc = jnp.concatenate([sc[:n], jnp.where(live, sc[n:], F32(-1e30))], axis=0)
        m = by_eight(sc).max(axis=0).max(axis=0, keepdims=True)
        e = jnp.exp2((sc - m) * SCALE_LOG2)
        e_buf[g, y0] = e
        dp_buf[g, y0] = dp
        stats[0, g, y0] = m
        stats[1, g, y0] = by_eight(e).sum(axis=0).sum(axis=0, keepdims=True)
        stats[2, g, y0] = by_eight(e * dp).sum(axis=0).sum(axis=0, keepdims=True)

    reach = ((4, 3), (3, 4))

    def hop_rows(hop):
        return (y + NY - hop) % NY, (y + hop) % NY

    def lead_hop(hop):
        for kv in range(2):
            for way, y0 in enumerate(hop_rows(hop)):
                if hop <= reach[kv][way]:
                    arrived(kv, 0, z, y0)
                    if hop < reach[kv][way]:
                        push(part(kv, 0, z, y0), kv, 0, z, y0, both[way])
                    for m in mates:
                        push(part(kv, 0, z, y0), kv, 0, z, y0, {"seq_0": m})

    def bulk_hop(hop, m):
        for kv in range(2):
            for way, y0 in enumerate(hop_rows(hop)):
                if hop <= reach[kv][way]:
                    arrived(kv, 1, m, y0)
                    if hop < reach[kv][way]:
                        push(part(kv, 1, m, y0), kv, 1, m, y0, both[way])

    def column(m):
        for kv in range(2):
            arrived(kv, 1, m, y)
            for target in both:
                push(part(kv, 1, m, y), kv, 1, m, y, target)

    def units_of(rows):
        for y0 in rows:
            for kv in range(2):
                for m in mates:
                    arrived(kv, 0, m, y0)
        return [(y0, g) for y0 in rows for g in range(GROUPS)]

    for i, m in enumerate(mates):
        lead_hop(i + 1)
        bulk_hop(i + 1, z)
        column(m)
    shift.wait_recv()
    for g in range(GROUPS):
        d2[g] = halves(d_new, g)
    lead_hop(4)
    bulk_hop(4, z)
    todo = [y]
    for hop in range(1, 5):
        bulk_hop(hop, mates[0])
        units = units_of(todo)
        for m in mates[1:] + (None,):
            for unit in units[:2]:
                scores_unit(*unit)
            units = units[2:]
            if m is not None:
                bulk_hop(hop, m)
        todo = hop_rows(hop) if hop < 4 else hop_rows(hop)[:1]
    for unit in units_of(todo):
        scores_unit(*unit)

    for g in range(GROUPS):
        m_c = [stats[0, g, c] for c in range(NY)]
        top = functools.reduce(jnp.maximum, m_c)
        f_c = [jnp.exp2((m - top) * SCALE_LOG2) for m in m_c]
        inv = 1.0 / sum(f * stats[1, g, c] for c, f in enumerate(f_c))
        delta = sum(f * stats[2, g, c] for c, f in enumerate(f_c)) * inv
        total = jnp.zeros((HD, q2.shape[1]), F32)
        for c in range(NY):
            p = e_buf[g, c] * (f_c[c] * inv)
            ds = (p * (dp_buf[g, c] - delta)).astype(BF16)
            p_buf[g, c] = p.astype(BF16)
            ds_buf[g, c] = ds
            total = total + dot_tn(chunk_of(k_all, c, g), ds)
        total = (SCALE * total).astype(BF16)
        half = total.shape[1] // 2
        gq[2 * g * HD : (2 * g + 1) * HD, :] = total[:, :half]
        gq[(2 * g + 1) * HD : (2 * g + 2) * HD, :] = total[:, half:]

    def gq_copy(end):
        return remote(
            gq, gq_in.at[z], gq_send.at[end], gq_recv.at[z], {"seq_0": z * 0 + end * (NZ - 1)}
        )

    def gq_leaves(distance):
        for end in range(2):
            @pl.when(z == end * (NZ - 1) + distance * (1 - 2 * end))
            def _():
                gq_copy(end).start()

    gq_leaves(2)
    gq_leaves(3)
    for copy in w_copies:
        copy.wait()

    def gi_copy(k):
        return remote(
            gi_send.at[k],
            gi_recv.at[1 - side],
            gi_ssem.at[k],
            gi_rsem.at[1 - side],
            far_goals[k - 1] if k else own_goal,
        )

    gi_send[0] = dot_nn(w_edge[...], gq[...]).astype(BF16)

    @pl.when(is_edge)
    def _():
        gi_copy(0).start()

    def edge_step(k):
        @pl.when(is_edge)
        def _():
            j = place(k + 1)
            remote(gq, gq_in.at[j], gq_send.at[0], gq_recv.at[j], {"seq_0": j}).wait_recv()
            gi_send[k] = dot_nn(w_edge[...], gq_in[j]).astype(BF16)
            gi_copy(k).start()

    terms = (gk, gv)
    chains = ((0, 1, 4, 0), (1, -1, 4, 4), (0, -1, 3, 8), (1, 1, 3, 11))
    ring_sent = []

    def ring_copy(chain, hop, src):
        kv, way, hops, slot = chain
        i = slot + hop
        return remote(src, ring.at[i], ring_send.at[i], ring_recv.at[i], both[0 if way > 0 else 1])

    def terms_unit(y0):
        for g in range(GROUPS):
            cols = slice(g * HD, (g + 1) * HD)
            gk[y0, :, cols] = (SCALE * dot_nn(ds_buf[g, y0], q2[g])).astype(BF16)
            gv[y0, :, cols] = dot_nn(p_buf[g, y0], d2[g]).astype(BF16)

    def ring_start(chain):
        kv, way, hops, slot = chain
        owner = (y + NY + way * hops) % NY
        copy = ring_copy(chain, 0, terms[kv].at[owner])
        copy.start()
        ring_sent.append(copy)

    terms_unit((y + 4) % NY)
    ring_start(chains[0])
    ring_start(chains[1])
    terms_unit((y + 3) % NY)
    ring_start(chains[3])
    terms_unit((y + 5) % NY)
    ring_start(chains[2])
    for d in (2, 6, 1, 7, 0):
        terms_unit((y + d) % NY)
    gi_own[...] = dot_nn(w_own[...], gq[...])

    @pl.when(jnp.logical_not(is_edge))
    def _():
        gi_copy(0).start()


    for hop in range(4):
        for at, chain in enumerate(chains):
            if at == 2 and hop in (1, 2):
                edge_step(hop)
            kv, way, hops, slot = chain
            if hop >= hops:
                continue
            i = slot + hop
            ring_copy(chain, hop, ring.at[i]).wait_recv()
            if hop < hops - 1:
                owner = (y + NY + way * (hops - 1 - hop)) % NY
                ring[i] = (ring[i].astype(F32) + terms[kv][owner].astype(F32)).astype(BF16)
                copy = ring_copy(chain, hop + 1, ring.at[i])
                copy.start()
                ring_sent.append(copy)
    ends = ((3, 10), (13, 7))
    line_copies = []
    for kv in range(2):
        a, b = ends[kv]
        mine[kv] = (
            (ring[a].astype(F32) + ring[b].astype(F32) + terms[kv][y].astype(F32))
            .astype(BF16)
            .reshape(mine.shape[1:])
        )
        for i, m in enumerate(mates):
            copy = remote(
                mine.at[kv, m], line.at[kv, i], line_send.at[kv, i], line_recv.at[kv, i], {"seq_0": m}
            )
            copy.start()
            line_copies.append(copy)
    for copy in line_copies:
        copy.wait_recv()
    out_copies = []
    for kv, out in enumerate((gk_out, gv_out)):
        gkv_fin[kv] = (
            mine[kv, z].astype(F32)
            + line[kv, 0].astype(F32)
            + line[kv, 1].astype(F32)
            + line[kv, 2].astype(F32)
        ).astype(BF16)
        out_copies.append(pltpu.make_async_copy(gkv_fin.at[kv], out, out_sem.at[kv]))
        out_copies[-1].start()
    for i in range(2):
        remote(
            gi_send.at[i], gi_recv.at[i], gi_ssem.at[i], gi_rsem.at[i], {"seq_1": right}
        ).wait_recv()
    gi_fin[...] = (gi_own[...] + gi_recv[0].astype(F32) + gi_recv[1].astype(F32)).astype(BF16)
    out_copies.append(pltpu.make_async_copy(gi_fin, gi_out, out_sem.at[2]))
    out_copies[-1].start()

    gather_rows = sum(n for n in sent) * k_ref.shape[1] // w_ref.shape[1]
    gather_all = w_ref.at[pl.ds(0, gather_rows), :]
    remote(gather_all, gather_all, send.at[0], misc.at[1], both[0]).wait_send()
    for copy in ring_sent + line_copies:
        copy.wait_send()
    shift.wait_send()
    for end in range(2):
        @pl.when(side != end)
        def _():
            gq_copy(end).wait_send()

    gi_copy(0).wait_send()

    @pl.when(is_edge)
    def _():
        for k in (1, 2):
            gi_copy(k).wait_send()

    for copy in out_copies:
        copy.wait()


def tick(span, prefix, q, d, k, v, w):
    rows, width = q.shape
    size, kv_width = k.shape
    features = w.shape[0] // NH
    chunk = NZ * size
    block = (NZ, size, kv_width)
    return pl.pallas_call(
        tick_kernel,
        out_shape=(
            jax.ShapeDtypeStruct((features, rows), BF16),
            jax.ShapeDtypeStruct(k.shape, BF16),
            jax.ShapeDtypeStruct(v.shape, BF16),
        ),
        in_specs=[pl.BlockSpec(memory_space=SMEM)] * 2
        + [pl.BlockSpec(memory_space=pl.ANY)] * 5,
        out_specs=(pl.BlockSpec(memory_space=pl.ANY),) * 3,
        scratch_shapes=[
            VMEM(q.shape, BF16),
            VMEM((features, rows), BF16),
            VMEM((2,) + k.shape, BF16),
            VMEM((NY,) + block, BF16),
            VMEM((NY,) + block, BF16),
            VMEM((rows, width), BF16),
            VMEM((GROUPS, 2 * rows, HD), BF16),
            VMEM((GROUPS, 2 * rows, HD), BF16),
            VMEM((features, width), BF16),
            VMEM((features, width), BF16),
            VMEM((GROUPS, NY, chunk, 2 * rows), F32),
            VMEM((GROUPS, NY, chunk, 2 * rows), F32),
            VMEM((3, GROUPS, NY, 1, 2 * rows), F32),
            VMEM((GROUPS, NY, chunk, 2 * rows), BF16),
            VMEM((GROUPS, NY, chunk, 2 * rows), BF16),
            VMEM((NY, chunk, kv_width), BF16),
            VMEM((NY, chunk, kv_width), BF16),
            VMEM((width, rows), BF16),
            VMEM((NZ, width, rows), BF16),
            VMEM((3, features, rows), BF16),
            VMEM((2, features, rows), BF16),
            VMEM((features, rows), F32),
            VMEM((14, chunk, kv_width), BF16),
            VMEM((2,) + block, BF16),
            VMEM((2, 3, size, kv_width), BF16),
            DMA((1,)),
            DMA((2, NY, NZ)),
            DMA((2, NY, NZ)),
            DMA((4,)),
            DMA((2,)),
            DMA((NZ,)),
            DMA((3,)),
            DMA((2,)),
            DMA((14,)),
            DMA((14,)),
            DMA((2, 3)),
            DMA((2, 3)),
            DMA((3,)),
            DMA((3,)),
        ],
        compiler_params=pltpu.CompilerParams(
            collective_id=0, has_side_effects=True, vmem_limit_bytes=60 * 1024 * 1024
        ),
        name="tick",
    )(span, prefix, q, d, k, v, w)


def hand_on_kernel(*refs):
    for src, dst in zip(refs[:3], refs[3:]):
        dst[...] = src[...]


def hand_on(*arrays):
    vmem = pl.BlockSpec(memory_space=VMEM)
    return pl.pallas_call(
        hand_on_kernel,
        out_shape=tuple(jax.ShapeDtypeStruct(a.shape, a.dtype) for a in arrays),
        in_specs=[vmem] * 3,
        out_specs=(vmem,) * 3,
        name="hand_on",
    )(*arrays)


def on_device(queries, grad_out, keys, values, proj_query, section_span, span_prefix):
    outs = tick(
        section_span, span_prefix, queries[0], grad_out[0], keys[0], values[0], proj_query[0]
    )
    return tuple(a[None] for a in hand_on(*outs))


def solution(mesh):
    split = Mesh(
        mesh.devices.reshape(mesh.shape["section"], NZ, NY, mesh.shape["head"]),
        ("section", "seq_0", "seq_1", "head"),
    )
    in_specs = (
        P("section", SEQ, "head"),
        P("section", SEQ, "head"),
        P("section", SEQ, "head"),
        P("section", SEQ, "head"),
        P("section", None, "head"),
        P(),
        P(),
    )
    out_specs = (P("section", "head", SEQ), P("section", SEQ, "head"), P("section", SEQ, "head"))
    return jax.shard_map(
        on_device, mesh=split, in_specs=in_specs, out_specs=out_specs, check_vma=False
    )
```

```python
import functools
import math

import jax
import jax.numpy as jnp
from jax import lax
from jax.experimental import pallas as pl
from jax.experimental.pallas import tpu as pltpu
from jax.sharding import Mesh
from jax.sharding import PartitionSpec as P

HD = 128
SEQ = ("seq_0", "seq_1")
NZ = 4
NY = 8
NS = 8
NH = 3
GROUPS = 3
SCALE = 168.0 ** (-0.5)
SCALE_LOG2 = SCALE * math.log2(math.e)
LEAD = 16
VMEM = pltpu.VMEM
SMEM = pltpu.SMEM
DMA = pltpu.SemaphoreType.DMA
BF16 = jnp.bfloat16
F32 = jnp.float32


def column_mates(z):
    return (z + 1 - 2 * (z % 2), (z + 2) % NZ, NZ - 1 - z)


def remote(src, dst, send, recv, target):
    return pltpu.make_async_remote_copy(
        src_ref=src,
        dst_ref=dst,
        send_sem=send,
        recv_sem=recv,
        device_id=target,
        device_id_type=pl.DeviceIdType.MESH,
    )


def dot_nt(a, b):
    return lax.dot_general(a, b, (((1,), (1,)), ((), ())), preferred_element_type=F32)


def dot_nn(a, b):
    return lax.dot_general(a, b, (((1,), (0,)), ((), ())), preferred_element_type=F32)


def dot_tn(a, b):
    return lax.dot_general(a, b, (((0,), (0,)), ((), ())), preferred_element_type=F32)


def by_eight(x):
    return x.reshape(x.shape[0] // 8, 8, x.shape[1])


def flat(x):
    return x.reshape(x.shape[0] * x.shape[1], x.shape[2])


def tick_kernel(
    span_ref, prefix_ref, q_hbm, d_ref, k_ref, v_ref, w_ref,
    gi_out, gk_out, gv_out,
    q_ref, gi_fin, gkv_fin, k_all, v_all, d_new, q2, d2, w_own, w_edge,
    e_buf, dp_buf, stats, ds_buf, p_buf, gk, gv,
    gq, gq_in, gi_send, gi_recv, gi_own, ring, mine, line,
    send, recv_a, recv_b, misc, gq_send, gq_recv, gi_ssem, gi_rsem,
    ring_send, ring_recv, line_send, line_recv, in_sem, out_sem,
):
    z = lax.axis_index("seq_0")
    y = lax.axis_index("seq_1")
    h = lax.axis_index("head")
    s = lax.axis_index("section")
    right, left = (y + 1) % NY, (y + NY - 1) % NY
    mates = column_mates(z)
    lower, upper = (s + NS - 1) % NS, (s + 1) % NS
    before, after = (h + NH - 1) % NH, (h + 1) % NH
    top_edge = z // (NZ - 1)
    is_edge = (z % (NZ - 1)) == 0
    side = z // 2
    goal = (h + NH - 1 + 2 * side) % NH

    def place(distance):
        return distance + top_edge * (NZ - 1 - 2 * distance)

    own_goal = {"seq_0": z, "head": goal}
    far_goals = [{"seq_0": place(distance), "head": goal} for distance in (2, 3)]

    barrier = pltpu.get_barrier_semaphore()

    def greet(target):
        pl.semaphore_signal(
            barrier, inc=1, device_id=target, device_id_type=pl.DeviceIdType.MESH
        )

    for target in (
        [{"seq_1": right}, {"seq_1": left}]
        + [{"seq_0": m} for m in mates]
        + [{"section": lower}, {"section": upper}]
        + [
            {"seq_0": z * side + (NZ - 1) * (1 - side), "head": before},
            {"seq_0": z * (1 - side), "head": after},
            own_goal,
        ]
    ):
        greet(target)

    @pl.when(is_edge)
    def _():
        for target in far_goals:
            greet(target)

    own = (k_ref, v_ref)
    full = (k_all, v_all)
    in_copies = [pltpu.make_async_copy(own[kv], full[kv].at[y, z], in_sem.at[kv]) for kv in range(2)]
    in_copies.append(pltpu.make_async_copy(q_hbm, q_ref, in_sem.at[2]))
    for copy in in_copies:
        copy.start()
    pl.semaphore_wait(barrier, 10 + 2 * jnp.where(is_edge, 1, 0))

    size = k_ref.shape[0]
    rows_of = (pl.ds(0, LEAD), pl.ds(LEAD, size - LEAD))
    sent = []

    def part(kv, cls, z0, y0):
        return full[kv].at[y0, z0, rows_of[cls]]

    def push(src, kv, cls, z0, y0, target):
        if cls == 0:
            sem = recv_a.at[1 if "seq_0" in target else 0, kv, y0]
        else:
            sem = recv_b.at[kv, y0, z0]
        copy = remote(src, part(kv, cls, z0, y0), send.at[0], sem, target)
        copy.start()
        sent.append(LEAD if cls == 0 else size - LEAD)

    def arrived(kv, cls, z0, y0):
        block = part(kv, cls, z0, y0)
        sem = recv_b.at[kv, y0, z0] if cls else recv_a.at[0, kv, y0]
        remote(block, block, send.at[0], sem, {"seq_1": right}).wait_recv()

    both = ({"seq_1": right}, {"seq_1": left})
    for kv in range(2):
        for target in both:
            push(own[kv].at[rows_of[0]], kv, 0, z, y, target)
    for m in mates:
        for kv in range(2):
            push(own[kv].at[rows_of[1]], kv, 1, z, y, {"seq_0": m})
    for kv in range(2):
        for target in both:
            push(own[kv].at[rows_of[1]], kv, 1, z, y, target)
    for m in mates:
        for kv in range(2):
            push(own[kv].at[rows_of[0]], kv, 0, z, y, {"seq_0": m})
    shift = remote(d_ref, d_new, misc.at[0], misc.at[1], {"section": lower})
    shift.start()
    w_size = w_own.shape[0]
    w_copies = [
        pltpu.make_async_copy(
            w_ref.at[pl.ds(pl.multiple_of(at * w_size, w_size), w_size), :], buf, misc.at[2 + i]
        )
        for i, (at, buf) in enumerate(((h, w_own), (goal, w_edge)))
    ]
    for copy in w_copies:
        copy.start()
    for copy in in_copies:
        copy.wait()

    length = prefix_ref[span_ref[s]]

    def halves(ref, g):
        return jnp.concatenate(
            [ref[:, 2 * g * HD : (2 * g + 1) * HD], ref[:, (2 * g + 1) * HD : (2 * g + 2) * HD]],
            axis=0,
        )

    for g in range(GROUPS):
        q2[g] = halves(q_ref, g)

    def chunk_of(ref, y0, g):
        return flat(ref[y0, :, :, g * HD : (g + 1) * HD])

    def scores_unit(y0, g):
        sc = dot_nt(chunk_of(k_all, y0, g), q2[g])
        dp = dot_nt(chunk_of(v_all, y0, g), d2[g])
        n = sc.shape[0] // 2
        i = lax.broadcasted_iota(jnp.int32, (n, sc.shape[1]), 0)
        t = i + jnp.where(i >= size, (NY - 1) * size, 0)
        live = t < length - 2 * NY * size - y0 * size
        sc = jnp.concatenate([sc[:n], jnp.where(live, sc[n:], F32(-1e30))], axis=0)
        m = by_eight(sc).max(axis=0).max(axis=0, keepdims=True)
        e = jnp.exp2((sc - m) * SCALE_LOG2)
        e_buf[g, y0] = e
        dp_buf[g, y0] = dp
        stats[0, g, y0] = m
        stats[1, g, y0] = by_eight(e).sum(axis=0).sum(axis=0, keepdims=True)
        stats[2, g, y0] = by_eight(e * dp).sum(axis=0).sum(axis=0, keepdims=True)

    reach = ((4, 3), (3, 4))

    def hop_rows(hop):
        return (y + NY - hop) % NY, (y + hop) % NY

    def lead_hop(hop):
        for kv in range(2):
            for way, y0 in enumerate(hop_rows(hop)):
                if hop <= reach[kv][way]:
                    arrived(kv, 0, z, y0)
                    if hop < reach[kv][way]:
                        push(part(kv, 0, z, y0), kv, 0, z, y0, both[way])
                    for m in mates:
                        push(part(kv, 0, z, y0), kv, 0, z, y0, {"seq_0": m})

    def bulk_hop(hop, m):
        for kv in range(2):
            for way, y0 in enumerate(hop_rows(hop)):
                if hop <= reach[kv][way]:
                    arrived(kv, 1, m, y0)
                    if hop < reach[kv][way]:
                        push(part(kv, 1, m, y0), kv, 1, m, y0, both[way])

    def column(m):
        for kv in range(2):
            arrived(kv, 1, m, y)
            for target in both:
                push(part(kv, 1, m, y), kv, 1, m, y, target)

    def units_of(rows):
        for y0 in rows:
            for kv in range(2):
                block = full[kv].at[y0, 0, pl.ds(0, 3 * LEAD)]
                remote(block, block, send.at[0], recv_a.at[1, kv, y0], both[0]).wait_recv()
        return [(y0, g) for y0 in rows for g in range(GROUPS)]

    for i, m in enumerate(mates):
        lead_hop(i + 1)
        bulk_hop(i + 1, z)
        column(m)
    shift.wait_recv()
    for g in range(GROUPS):
        d2[g] = halves(d_new, g)
    lead_hop(4)
    bulk_hop(4, z)
    todo = [y]
    for hop in range(1, 5):
        bulk_hop(hop, mates[0])
        units = units_of(todo)
        for m in mates[1:] + (None,):
            for unit in units[:2]:
                scores_unit(*unit)
            units = units[2:]
            if m is not None:
                bulk_hop(hop, m)
        todo = hop_rows(hop) if hop < 4 else hop_rows(hop)[:1]
    for unit in units_of(todo):
        scores_unit(*unit)

    for g in range(GROUPS):
        m_c = [stats[0, g, c] for c in range(NY)]
        top = functools.reduce(jnp.maximum, m_c)
        f_c = [jnp.exp2((m - top) * SCALE_LOG2) for m in m_c]
        inv = 1.0 / sum(f * stats[1, g, c] for c, f in enumerate(f_c))
        delta = sum(f * stats[2, g, c] for c, f in enumerate(f_c)) * inv
        total = jnp.zeros((HD, q2.shape[1]), F32)
        for c in range(NY):
            p = e_buf[g, c] * (f_c[c] * inv)
            ds = (p * (dp_buf[g, c] - delta)).astype(BF16)
            p_buf[g, c] = p.astype(BF16)
            ds_buf[g, c] = ds
            total = total + dot_tn(chunk_of(k_all, c, g), ds)
        total = (SCALE * total).astype(BF16)
        half = total.shape[1] // 2
        gq[2 * g * HD : (2 * g + 1) * HD, :] = total[:, :half]
        gq[(2 * g + 1) * HD : (2 * g + 2) * HD, :] = total[:, half:]

    def gq_copy(end):
        return remote(
            gq, gq_in.at[z], gq_send.at[end], gq_recv.at[z], {"seq_0": z * 0 + end * (NZ - 1)}
        )

    def gq_leaves(distance):
        for end in range(2):
            @pl.when(z == end * (NZ - 1) + distance * (1 - 2 * end))
            def _():
                gq_copy(end).start()

    gq_leaves(2)
    gq_leaves(3)
    for copy in w_copies:
        copy.wait()

    def gi_copy(k):
        return remote(
            gi_send.at[k],
            gi_recv.at[1 - side],
            gi_ssem.at[k],
            gi_rsem.at[1 - side],
            far_goals[k - 1] if k else own_goal,
        )

    gi_send[0] = dot_nn(w_edge[...], gq[...]).astype(BF16)

    @pl.when(is_edge)
    def _():
        gi_copy(0).start()

    def edge_step(k):
        @pl.when(is_edge)
        def _():
            j = place(k + 1)
            remote(gq, gq_in.at[j], gq_send.at[0], gq_recv.at[j], {"seq_0": j}).wait_recv()
            gi_send[k] = dot_nn(w_edge[...], gq_in[j]).astype(BF16)
            gi_copy(k).start()

    terms = (gk, gv)
    chains = ((0, 1, 4, 0), (1, -1, 4, 4), (0, -1, 3, 8), (1, 1, 3, 11))
    ring_sent = []

    def ring_copy(chain, hop, src):
        kv, way, hops, slot = chain
        i = slot + hop
        return remote(src, ring.at[i], ring_send.at[0], ring_recv.at[i], both[0 if way > 0 else 1])

    def terms_unit(y0):
        for g in range(GROUPS):
            cols = slice(g * HD, (g + 1) * HD)
            gk[y0, :, cols] = (SCALE * dot_nn(ds_buf[g, y0], q2[g])).astype(BF16)
            gv[y0, :, cols] = dot_nn(p_buf[g, y0], d2[g]).astype(BF16)

    def ring_start(chain):
        kv, way, hops, slot = chain
        owner = (y + NY + way * hops) % NY
        copy = ring_copy(chain, 0, terms[kv].at[owner])
        copy.start()
        ring_sent.append(copy)

    terms_unit((y + 4) % NY)
    ring_start(chains[0])
    ring_start(chains[1])
    terms_unit((y + 3) % NY)
    ring_start(chains[3])
    terms_unit((y + 5) % NY)
    ring_start(chains[2])
    for d in (2, 6, 1, 7, 0):
        terms_unit((y + d) % NY)
    gi_own[...] = dot_nn(w_own[...], gq[...])

    @pl.when(jnp.logical_not(is_edge))
    def _():
        gi_copy(0).start()


    for hop in range(4):
        for at, chain in enumerate(chains):
            if at == 2 and hop in (1, 2):
                edge_step(hop)
            kv, way, hops, slot = chain
            if hop >= hops:
                continue
            i = slot + hop
            ring_copy(chain, hop, ring.at[i]).wait_recv()
            if hop < hops - 1:
                owner = (y + NY + way * (hops - 1 - hop)) % NY
                ring[i] = (ring[i].astype(F32) + terms[kv][owner].astype(F32)).astype(BF16)
                copy = ring_copy(chain, hop + 1, ring.at[i])
                copy.start()
                ring_sent.append(copy)
    ends = ((3, 10), (13, 7))
    line_copies = []
    for kv in range(2):
        a, b = ends[kv]
        mine[kv] = (
            (ring[a].astype(F32) + ring[b].astype(F32) + terms[kv][y].astype(F32))
            .astype(BF16)
            .reshape(mine.shape[1:])
        )
        for i, m in enumerate(mates):
            copy = remote(
                mine.at[kv, m], line.at[kv, i], line_send.at[0], line_recv.at[kv, i], {"seq_0": m}
            )
            copy.start()
            line_copies.append(copy)
    for copy in line_copies:
        copy.wait_recv()
    out_copies = []
    for kv, out in enumerate((gk_out, gv_out)):
        gkv_fin[kv] = (
            mine[kv, z].astype(F32)
            + line[kv, 0].astype(F32)
            + line[kv, 1].astype(F32)
            + line[kv, 2].astype(F32)
        ).astype(BF16)
        out_copies.append(pltpu.make_async_copy(gkv_fin.at[kv], out, out_sem.at[kv]))
        out_copies[-1].start()
    for i in range(2):
        remote(
            gi_send.at[i], gi_recv.at[i], gi_ssem.at[i], gi_rsem.at[i], {"seq_1": right}
        ).wait_recv()
    gi_fin[...] = (gi_own[...] + gi_recv[0].astype(F32) + gi_recv[1].astype(F32)).astype(BF16)
    out_copies.append(pltpu.make_async_copy(gi_fin, gi_out, out_sem.at[2]))
    out_copies[-1].start()

    gather_rows = sum(n for n in sent) * k_ref.shape[1] // w_ref.shape[1]
    gather_all = w_ref.at[pl.ds(0, gather_rows), :]
    remote(gather_all, gather_all, send.at[0], misc.at[1], both[0]).wait_send()
    remote(ring, ring, ring_send.at[0], ring_recv.at[0], both[0]).wait_send()
    remote(line, line, line_send.at[0], line_recv.at[0, 0], both[0]).wait_send()
    shift.wait_send()
    for end in range(2):
        @pl.when(side != end)
        def _():
            gq_copy(end).wait_send()

    gi_copy(0).wait_send()

    @pl.when(is_edge)
    def _():
        for k in (1, 2):
            gi_copy(k).wait_send()

    for copy in out_copies:
        copy.wait()


def tick(span, prefix, q, d, k, v, w):
    rows, width = q.shape
    size, kv_width = k.shape
    features = w.shape[0] // NH
    chunk = NZ * size
    block = (NZ, size, kv_width)
    return pl.pallas_call(
        tick_kernel,
        out_shape=(
            jax.ShapeDtypeStruct((features, rows), BF16),
            jax.ShapeDtypeStruct(k.shape, BF16),
            jax.ShapeDtypeStruct(v.shape, BF16),
        ),
        in_specs=[pl.BlockSpec(memory_space=SMEM)] * 2
        + [pl.BlockSpec(memory_space=pl.ANY)] * 5,
        out_specs=(pl.BlockSpec(memory_space=pl.ANY),) * 3,
        scratch_shapes=[
            VMEM(q.shape, BF16),
            VMEM((features, rows), BF16),
            VMEM((2,) + k.shape, BF16),
            VMEM((NY,) + block, BF16),
            VMEM((NY,) + block, BF16),
            VMEM((rows, width), BF16),
            VMEM((GROUPS, 2 * rows, HD), BF16),
            VMEM((GROUPS, 2 * rows, HD), BF16),
            VMEM((features, width), BF16),
            VMEM((features, width), BF16),
            VMEM((GROUPS, NY, chunk, 2 * rows), F32),
            VMEM((GROUPS, NY, chunk, 2 * rows), F32),
            VMEM((3, GROUPS, NY, 1, 2 * rows), F32),
            VMEM((GROUPS, NY, chunk, 2 * rows), BF16),
            VMEM((GROUPS, NY, chunk, 2 * rows), BF16),
            VMEM((NY, chunk, kv_width), BF16),
            VMEM((NY, chunk, kv_width), BF16),
            VMEM((width, rows), BF16),
            VMEM((NZ, width, rows), BF16),
            VMEM((3, features, rows), BF16),
            VMEM((2, features, rows), BF16),
            VMEM((features, rows), F32),
            VMEM((14, chunk, kv_width), BF16),
            VMEM((2,) + block, BF16),
            VMEM((2, 3, size, kv_width), BF16),
            DMA((1,)),
            DMA((2, 2, NY)),
            DMA((2, NY, NZ)),
            DMA((4,)),
            DMA((2,)),
            DMA((NZ,)),
            DMA((3,)),
            DMA((2,)),
            DMA((1,)),
            DMA((14,)),
            DMA((1,)),
            DMA((2, 3)),
            DMA((3,)),
            DMA((3,)),
        ],
        compiler_params=pltpu.CompilerParams(
            collective_id=0, has_side_effects=True, vmem_limit_bytes=60 * 1024 * 1024
        ),
        name="tick",
    )(span, prefix, q, d, k, v, w)


def hand_on_kernel(*refs):
    for src, dst in zip(refs[:3], refs[3:]):
        dst[...] = src[...]


def hand_on(*arrays):
    vmem = pl.BlockSpec(memory_space=VMEM)
    return pl.pallas_call(
        hand_on_kernel,
        out_shape=tuple(jax.ShapeDtypeStruct(a.shape, a.dtype) for a in arrays),
        in_specs=[vmem] * 3,
        out_specs=(vmem,) * 3,
        name="hand_on",
    )(*arrays)


def on_device(queries, grad_out, keys, values, proj_query, section_span, span_prefix):
    outs = tick(
        section_span, span_prefix, queries[0], grad_out[0], keys[0], values[0], proj_query[0]
    )
    return tuple(a[None] for a in hand_on(*outs))


def solution(mesh):
    split = Mesh(
        mesh.devices.reshape(mesh.shape["section"], NZ, NY, mesh.shape["head"]),
        ("section", "seq_0", "seq_1", "head"),
    )
    in_specs = (
        P("section", SEQ, "head"),
        P("section", SEQ, "head"),
        P("section", SEQ, "head"),
        P("section", SEQ, "head"),
        P("section", None, "head"),
        P(),
        P(),
    )
    out_specs = (P("section", "head", SEQ), P("section", SEQ, "head"), P("section", SEQ, "head"))
    return jax.shard_map(
        on_device, mesh=split, in_specs=in_specs, out_specs=out_specs, check_vma=False
    )
```
